128 devices in a mesh: sens: 8 (over z, core), layer: 16 (over y, x).
Axes of the slice: x: 4, y: 4, z: 4, core: 2. Of those that a mesh axis runs over, the one named last changes fastest.
Arguments:
- slopes: bfloat16 [1024, 63600], P('layer', 'sens'), may hold values from -7 to 7
- valid: int32 [63600], P('sens'), may hold values from 0 to 1
- sensor_map: int32 [63600], P('sens'), may hold values from 0 to 5, as said below
- reconstructor: bfloat16 [16000, 63600], P('layer', 'sens'), may hold values from -0.0234375 to 0.0234375
- fitting: bfloat16 [7800, 16000], P('sens', 'layer'), may hold values from -0.046875 to 0.046875
Outputs:
- commands: float32 [1024, 7800], P(('sens', 'layer'))
The draws below stay inside these ranges and needn't reach their ends.
Inputs may be any that keep to these rules, and one draw needn't show every extreme that they name: `sensor_map`: both slopes of a subaperture (indices 2 i and 2 i + 1) belong to one sensor.
All inputs are finite; a program needn't handle non-finite values.
Results may differ from the reference program's by a relative error of at most 0.02.
Values may be sent and summed in bfloat16 or wider, within the bound.
No kernel may reach another device: no remote copies, remote signals or barrier semaphores. Data moves between devices by JAX's collectives and lax.ppermute only.
A program may use at most 192 MiB of HBM per device.

```python
import jax
import jax.numpy as jnp
from jax import lax

S = 63600
SENSORS = 6
P_SIZE = 16000
ACT = 7800
FRAMES = 1024
N_LAYER = 16


def draw_slopes(key, part):
    key_offset, key_noise = jax.random.split(jax.random.fold_in(key, 11), 2)
    offsets = jax.random.uniform(key_offset, (FRAMES, 16), jnp.float32, -3.0, 3.0)
    column = jnp.arange(S, dtype=jnp.int32) * 16 // S
    spread = offsets[:, column]
    noise = jnp.clip(jax.random.normal(key_noise, (FRAMES, S), jnp.float32), -3.5, 3.5)
    return (spread + noise).astype(jnp.bfloat16)


def sensor_layout(key):
    base = jax.random.fold_in(key, 23)
    key_pair, key_mask, key_lost = jax.random.split(base, 3)
    pair_sensor = jax.random.randint(key_pair, (S // 2,), 0, SENSORS, jnp.int32)
    sensor_map = jnp.repeat(pair_sensor, 2).astype(jnp.int32)
    mask = (jax.random.randint(key_mask, (S,), 0, 10, jnp.int32) < 9).astype(jnp.int32)
    lost = jax.random.randint(key_lost, (), 0, SENSORS, jnp.int32)
    valid = jnp.where(sensor_map == lost, 0, mask).astype(jnp.int32)
    return (sensor_map, valid)


def draw_sensor_map(key, part):
    return sensor_layout(key)[0]


def draw_valid(key, part):
    return sensor_layout(key)[1]


def steps_of(rng, extent, pieces, smallest, high):
    factor_of = 1.0
    for position, shards_of in pieces:
        heights = jax.random.uniform(jax.random.fold_in(jax.random.fold_in(rng, 6), position), (shards_of,), jnp.float32, smallest / len(pieces), high / len(pieces))
        factor_of = factor_of * jnp.repeat(jnp.exp(heights), extent[position] // shards_of).reshape((-1,) + (1,) * (len(extent) - 1 - position))
    return factor_of


def centred(rng, dims, width, most, shards=(), kind=jnp.bfloat16):
    result = jax.random.normal(rng, dims, jnp.float32) * width
    if len(shards) > 0:
        result = steps_of(rng, dims, shards, -0.22, 0.18) * result
    return jnp.clip(result, min=-most, max=most).astype(kind)


def setup_inputs(seed: int = 0) -> dict:
    seeds = jax.random.split(jax.random.key(seed), 6)
    slopes = draw_slopes(jax.random.fold_in(seeds[5], 71), 0)
    valid = draw_valid(jax.random.fold_in(seeds[5], 71), 0)
    sensor_map = draw_sensor_map(jax.random.fold_in(seeds[5], 71), 0)
    reconstructor = centred(seeds[3], (P_SIZE, S), S ** -0.5, 0.0234375, ((0, 16), (1, 8)))
    fitting = centred(seeds[4], (ACT, P_SIZE), P_SIZE ** -0.5, 0.046875, ((0, 8), (1, 16)))
    return dict(slopes=slopes, valid=valid, sensor_map=sensor_map, reconstructor=reconstructor, fitting=fitting)


def reference(slopes, valid, sensor_map, reconstructor, fitting):
    parity = jnp.arange(S, dtype=jnp.int32) % 2
    group = sensor_map * 2 + parity
    onehot = (group[:, None] == jnp.arange(2 * SENSORS, dtype=jnp.int32)[None, :]).astype(jnp.float32)
    live = valid.astype(jnp.float32)
    masked = slopes.astype(jnp.float32) * live[None, :]
    sums = jnp.dot(masked, onehot, precision=lax.Precision.HIGHEST)
    counts = jnp.dot(live, onehot, precision=lax.Precision.HIGHEST)
    means = sums / jnp.maximum(counts, 1.0)
    clean = (live[None, :] * (slopes.astype(jnp.float32) - means[:, group])).astype(jnp.bfloat16)
    blocks = reconstructor.reshape(N_LAYER, P_SIZE // N_LAYER, S)

    def project(block):
        return lax.dot_general(clean, block, (((1,), (1,)), ((), ())), preferred_element_type=jnp.float32)

    parts = lax.map(project, blocks)
    points = jnp.transpose(parts, (1, 0, 2)).reshape(FRAMES, P_SIZE).astype(jnp.bfloat16)
    commands = lax.dot_general(points, fitting, (((1,), (1,)), ((), ())), preferred_element_type=jnp.float32)
    return commands
```

```python
import functools

import jax
import jax.numpy as jnp
import numpy as np
from jax import lax
from jax.experimental import pallas as pl
from jax.experimental.pallas import tpu as pltpu
from jax.sharding import PartitionSpec as P

SENSORS = 6
GROUPS = 2 * SENSORS
AXES = ("sens", "layer")
SIDE = 4
ROWS = 64
QUARTER = 2048
LAST = 1920
PBLOCK = 256


def moved(fn):
    pairs = []
    for z in range(4):
        for c in range(2):
            for y in range(4):
                for x in range(4):
                    z2, c2, y2, x2 = fn(z, c, y, x)
                    pairs.append(
                        ((z * 2 + c) * 16 + y * 4 + x,
                         ((z2 % 4) * 2 + c2 % 2) * 16 + (y2 % 4) * 4 + x2 % 4)
                    )
    return pairs


def send(x, fn):
    return lax.ppermute(x, AXES, moved(fn))


def ring_x(v):
    return send(v, lambda z, c, y, x: (z, c, y, x + 1 - 2 * c))


def ring_y(v):
    return send(v, lambda z, c, y, x: (z, c, y + 1 - 2 * c, x))


def ring(v, step):
    held = [v]
    for _ in range(3):
        held.append(step(held[-1]))
    return held


def nt(a, b):
    return lax.dot_general(a, b, (((1,), (1,)), ((), ())), preferred_element_type=jnp.float32)


def mm_kernel(first, idx, x0, x1, r, *rest):
    if first:
        acc, out = rest
        val = nt(x0[...], r[:, :QUARTER]) + nt(x1[...], r[:, QUARTER:])
    else:
        rw, acc, out = rest
        cut = LAST - 128
        lane = lax.broadcasted_iota(jnp.int32, (r.shape[0], 128), 1)
        edge = r[:, QUARTER + cut : QUARTER + LAST]
        edge = jnp.where(lane < 14, edge.astype(jnp.float32), 0.0).astype(jnp.bfloat16)
        tail = x1[:, cut:]
        val = nt(x0[...], r[:, :QUARTER]) + nt(x1[:, :cut], r[:, QUARTER : QUARTER + cut])
        val = val + nt(tail, edge)
        val = val + lax.dot_general(
            tail.astype(jnp.float32), rw[...], (((1,), (1,)), ((), ())),
            preferred_element_type=jnp.float32, precision=lax.Precision.HIGHEST,
        )
    for u in range(SIDE):
        part = val[u * ROWS : (u + 1) * ROWS]
        w = idx[1 + u]
        if first:
            out[0, w] = acc[0, w] + part
        else:
            out[w, 0] = acc[w, 0] + part


def accumulate(first, idx, x0, x1, r, rw, acc):
    n = SIDE * ROWS
    blocks = pl.cdiv(r.shape[0], PBLOCK)
    half = 0 if first else 1
    if first:
        acc_spec = pl.BlockSpec((1, SIDE, ROWS, PBLOCK), lambda j, i: (i[0], 0, 0, j))
    else:
        acc_spec = pl.BlockSpec((SIDE, 1, ROWS, PBLOCK), lambda j, i: (0, i[0], 0, j))
    specs = [
        pl.BlockSpec((n, x0.shape[1]), lambda j, i: (0, 0)),
        pl.BlockSpec((n, x1.shape[1]), lambda j, i: (0, 0)),
        pl.BlockSpec((PBLOCK, 2 * QUARTER), lambda j, i: (j, half)),
    ]
    args = [x0, x1, r]
    if not first:
        specs.append(pl.BlockSpec((PBLOCK, 128), lambda j, i: (j, 0)))
        args.append(rw)
    specs.append(acc_spec)
    args.append(acc)
    return pl.pallas_call(
        functools.partial(mm_kernel, first),
        grid_spec=pltpu.PrefetchScalarGridSpec(
            num_scalar_prefetch=1, grid=(blocks,), in_specs=specs, out_specs=acc_spec
        ),
        out_shape=jax.ShapeDtypeStruct(acc.shape, acc.dtype),
        input_output_aliases={len(args): 0},
        compiler_params=pltpu.CompilerParams(vmem_limit_bytes=40 * 2**20),
        cost_estimate=pl.CostEstimate(
            flops=2 * n * 4096 * 1000, bytes_accessed=12 * 2**20, transcendentals=0
        ),
    )(idx, *args)


def fit_kernel(p, f, out):
    out[0] = nt(p[...], f[0]).astype(jnp.bfloat16)


def fit(points, fitting, start, count):
    n, k = points.shape
    m = fitting.shape[1]
    return pl.pallas_call(
        fit_kernel,
        grid=(count,),
        in_specs=[
            pl.BlockSpec((n, k), lambda s: (0, 0)),
            pl.BlockSpec((1, m, k), lambda s: (s + start, 0, 0)),
        ],
        out_specs=pl.BlockSpec((1, n, m), lambda s: (s, 0, 0)),
        out_shape=jax.ShapeDtypeStruct((count, n, m), jnp.bfloat16),
        compiler_params=pltpu.CompilerParams(vmem_limit_bytes=40 * 2**20),
        cost_estimate=pl.CostEstimate(
            flops=2 * n * m * k * count, bytes_accessed=2 * count * m * k, transcendentals=0
        ),
    )(points, fitting)


def summed(blocks, mine, hop, size):
    def pick(d):
        return lax.dynamic_index_in_dim(blocks, (mine + d) % size, 0, keepdims=False)

    got = [send(pick(d).astype(jnp.bfloat16), hop(d)) for d in (1, 3, 2)]
    total = pick(0).astype(jnp.float32)
    for g in got:
        total = total + g.astype(jnp.float32)
    return total


def per_device(slopes, valid, sensor_map, reconstructor, fitting):
    s_idx = lax.axis_index("sens")
    l_idx = lax.axis_index("layer")
    z, c = s_idx // 2, s_idx % 2
    y, x = l_idx // 4, l_idx % 4
    width = slopes.shape[1]
    sign = 1 - 2 * c
    spread = jnp.arange(SIDE, dtype=jnp.int32)
    ys = (y - sign * spread + 4) % 4
    xs = (x - sign * spread + 4) % 4

    everything = lax.all_gather(fitting, "sens", axis=0)

    masked = slopes * valid.astype(jnp.bfloat16)[None, :]
    group = sensor_map * 2 + (lax.iota(jnp.int32, width) + s_idx * width) % 2
    lane = lax.iota(jnp.int32, 128)
    label = jnp.where(lane < 26, lane - 14, lane - 26)
    label = jnp.where((lane >= 14) & (lane < 38), label, -1)
    member = ((group[None, :] == label[:, None]) & (valid[None, :] == 1)).astype(jnp.bfloat16)

    x_first = [masked[:, :QUARTER], masked[:, QUARTER : 2 * QUARTER]]
    y_first = [masked[:, 2 * QUARTER : 3 * QUARTER]]

    sums = nt(masked, member)
    counts = jnp.sum(member.astype(jnp.float32), axis=1)
    stats = jnp.concatenate([sums, jnp.broadcast_to(counts[None], (8, 128))], axis=0)
    stats = stats + send(stats, lambda z, c, y, x: (z, c + 1, y, x))
    others = [send(stats, lambda z, c, y, x, d=d: (z + d, c, y, x)) for d in (1, 3, 2)]
    stats = (stats + others[2]) + (others[0] + others[1])
    means = stats[:ROWS] / jnp.maximum(stats[ROWS:ROWS + 1], 1.0)
    high = lax.reduce_precision(means, 8, 7)
    low = means - high
    rows = jnp.where(lane[None, :] < 26, high, low)
    rows = jnp.where((lane[None, :] >= 14) & (lane[None, :] < 38), rows, 0.0).astype(jnp.bfloat16)
    last = masked[:, 3 * QUARTER :]
    last = jnp.pad(last, ((0, 0), (0, LAST - last.shape[1])))
    last = last + jnp.pad(rows, ((0, 0), (LAST - 128, 0)))
    y_first.append(last)

    rw = -nt(reconstructor, member)

    def gathered(v, one, two):
        block = jnp.concatenate(ring(v, one), axis=0)
        return ring(block, two)

    a = [gathered(v, ring_x, ring_y) for v in x_first]
    b = [gathered(v, ring_y, ring_x) for v in y_first]

    acc = jnp.zeros((SIDE, SIDE, ROWS, reconstructor.shape[0]), jnp.float32)
    for t in range(SIDE):
        ia = jnp.concatenate([ys[t : t + 1], xs])
        acc = accumulate(True, ia, a[0][t], a[1][t], reconstructor, None, acc)
        ib = jnp.concatenate([xs[t : t + 1], ys])
        acc = accumulate(False, ib, b[0][t], b[1][t], reconstructor, rw, acc)

    width_p = reconstructor.shape[0]
    cores = acc.reshape(SIDE, 2, 2 * ROWS, width_p)
    other = lax.dynamic_index_in_dim(cores, 1 - c, 1, keepdims=False).astype(jnp.bfloat16)
    mine = lax.dynamic_index_in_dim(cores, c, 1, keepdims=False)
    arrived = send(other, lambda z, c, y, x: (z, c + 1, y, x))
    layers = mine + arrived.astype(jnp.float32)
    points = summed(layers, z, lambda d: lambda z, c, y, x: (z + d, c, y, x), 4)
    points = points.astype(jnp.bfloat16)

    def hop_y(d):
        return lambda z, c, y, x: (z, c, y + d, x)

    def hop_x(d):
        return lambda z, c, y, x: (z, c, y, x + d)

    act = fitting.shape[0]
    out_a = fit(points, everything, 0, 4).reshape(4, 4, 4, 8, act)
    out_b = fit(points, everything, 4, 4).reshape(4, 4, 4, 8, act)
    part_a = summed(jnp.moveaxis(out_a, 1, 0), y, hop_y, 4)
    part_b = summed(jnp.moveaxis(out_b, 2, 0), x, hop_x, 4)
    done_a = summed(jnp.moveaxis(part_a, 1, 0), x, hop_x, 4)
    done_b = summed(jnp.moveaxis(part_b, 1, 0), y, hop_y, 4)
    done = jnp.concatenate([done_a, done_b], axis=0)
    return jnp.moveaxis(done, 0, 1).reshape(8, 8 * act)


def solution(mesh):
    placed = (P("layer", "sens"), P("sens"), P("sens"), P("layer", "sens"), P("sens", "layer"))
    return jax.shard_map(
        per_device,
        mesh=mesh,
        in_specs=placed,
        out_specs=P(("sens", "layer"), None),
        check_vma=False,
    )
```

```python
import functools

import jax
import jax.numpy as jnp
from jax import lax
from jax.experimental import pallas as pl
from jax.experimental.pallas import tpu as pltpu
from jax.sharding import PartitionSpec as P

SENSORS = 6
AXES = ("sens", "layer")
SIDE = 4
ROWS = 64
CUTS = (32, 32)
HALF = 4096
BWIDTH = 3968
EDGE = BWIDTH - 128
INSIDE = 14
SPAN = 24
PBLOCK = 256
VMEM = 48 * 2**20


def moved(fn):
    pairs = []
    for z in range(4):
        for c in range(2):
            for y in range(4):
                for x in range(4):
                    z2, c2, y2, x2 = fn(z, c, y, x)
                    pairs.append(
                        ((z * 2 + c) * 16 + y * 4 + x,
                         ((z2 % 4) * 2 + c2 % 2) * 16 + (y2 % 4) * 4 + x2 % 4)
                    )
    return pairs


def send(x, fn):
    return lax.ppermute(x, AXES, moved(fn))


def ring_x(v):
    return send(v, lambda z, c, y, x: (z, c, y, x + 1 - 2 * c))


def ring_y(v):
    return send(v, lambda z, c, y, x: (z, c, y + 1 - 2 * c, x))


def swap_core(v):
    return send(v, lambda z, c, y, x: (z, c + 1, y, x))


def hop_z(d):
    return lambda z, c, y, x: (z + d, c, y, x)


def hop_one(d):
    return lambda z, c, y, x: (z, c, y + d * (1 - c), x + d * c)


def hop_two(d):
    return lambda z, c, y, x: (z, c, y + d * c, x + d * (1 - c))


def after(value, *others):
    return lax.optimization_barrier((value, *others))


def nt(a, b, **kw):
    return lax.dot_general(
        a, b, (((1,), (1,)), ((), ())), preferred_element_type=jnp.float32, **kw
    )


def place(first, t, u):
    s_idx, l_idx = lax.axis_index("sens"), lax.axis_index("layer")
    core = lax.rem(s_idx, 2)
    sign = 1 - 2 * core
    ry, rx = (t, u) if first else (u, t)
    y = lax.rem(l_idx // SIDE - sign * ry + SIDE, SIDE)
    x = lax.rem(lax.rem(l_idx, SIDE) - sign * rx + SIDE, SIDE)
    other = lax.rem(x // 2 + core, 2)
    return other * 8 + y * 2 + lax.rem(x, 2)


def fetches(first, size, blocks, held, sems):
    copies = []
    for t in range(SIDE):
        for u in range(SIDE):
            row = pl.multiple_of(place(first, t, u) * size, size)
            copies.append(
                pltpu.make_async_copy(
                    blocks[t].at[pl.ds(u * size, size)],
                    held.at[pl.ds(row, size)],
                    sems.at[t * SIDE + u],
                )
            )
    return copies


def load(first, size, blocks, held, sems):
    @pl.when(pl.program_id(0) == 0)
    def _():
        copies = fetches(first, size, blocks, held, sems)
        for copy in copies:
            copy.start()
        for copy in copies:
            copy.wait()


def kernel_a(size, x0, x1, x2, x3, r, out, held, sems):
    load(True, size, (x0, x1, x2, x3), held, sems)
    out[...] = nt(held[...], r[...])


def kernel_b(size, index, x0, x1, x2, x3, r, rw, acc, *rest):
    if index == 0:
        own, other, tail_out, held, sems = rest
    else:
        tail_in, own, other, held, sems = rest
    load(False, size, (x0, x1, x2, x3), held, sems)
    lane = lax.broadcasted_iota(jnp.int32, (r.shape[0], 128), 1)
    edge = r[:, EDGE:BWIDTH].astype(jnp.float32)
    edge = jnp.where(lane < INSIDE, edge, 0.0).astype(jnp.bfloat16)
    tail = held[:, EDGE:]
    val = acc[...] + nt(held[:, :EDGE], r[:, :EDGE]) + nt(tail, edge)
    if index == 0:
        means = tail
        tail_out[...] = tail
    else:
        means = tail_in[...]
    val = val + nt(means.astype(jnp.float32), rw[...], precision=lax.Precision.HIGHEST)
    half = val.shape[0] // 2
    own[...] = val[:half]
    other[...] = val[half:].astype(jnp.bfloat16)


ANY = pl.BlockSpec(memory_space=pl.ANY)


def matmul_a(size, blocks, r):
    n = 16 * size
    p = r.shape[0]
    return pl.pallas_call(
        functools.partial(kernel_a, size),
        grid=(pl.cdiv(p, PBLOCK),),
        in_specs=[ANY] * 4 + [pl.BlockSpec((PBLOCK, HALF), lambda j: (j, 0))],
        out_specs=pl.BlockSpec((n, PBLOCK), lambda j: (0, j)),
        out_shape=jax.ShapeDtypeStruct((n, p), jnp.float32),
        scratch_shapes=[pltpu.VMEM((n, HALF), jnp.bfloat16), pltpu.SemaphoreType.DMA((16,))],
        compiler_params=pltpu.CompilerParams(vmem_limit_bytes=VMEM),
        cost_estimate=pl.CostEstimate(
            flops=3 * 2 * n * HALF * p, bytes_accessed=16 * 2**20, transcendentals=0
        ),
    )(*blocks, r)


def matmul_b(size, index, blocks, r, rw, acc, tail):
    n = 16 * size
    p = r.shape[0]
    specs = [ANY] * 4 + [
        pl.BlockSpec((PBLOCK, HALF), lambda j: (j, 1)),
        pl.BlockSpec((PBLOCK, 128), lambda j: (j, 0)),
        pl.BlockSpec((n, PBLOCK), lambda j: (0, j)),
    ]
    args = [*blocks, r, rw, acc]
    half_spec = pl.BlockSpec((n // 2, PBLOCK), lambda j: (0, j))
    whole = pl.BlockSpec((n, 128), lambda j: (0, 0))
    outs = [half_spec, half_spec]
    shapes = [
        jax.ShapeDtypeStruct((n // 2, p), jnp.float32),
        jax.ShapeDtypeStruct((n // 2, p), jnp.bfloat16),
    ]
    if index == 0:
        outs.append(whole)
        shapes.append(jax.ShapeDtypeStruct((n, 128), jnp.bfloat16))
    else:
        specs.append(whole)
        args.append(tail)
    return pl.pallas_call(
        functools.partial(kernel_b, size, index),
        grid=(pl.cdiv(p, PBLOCK),),
        in_specs=specs,
        out_specs=outs,
        out_shape=shapes,
        scratch_shapes=[pltpu.VMEM((n, BWIDTH), jnp.bfloat16), pltpu.SemaphoreType.DMA((16,))],
        compiler_params=pltpu.CompilerParams(vmem_limit_bytes=VMEM),
        cost_estimate=pl.CostEstimate(
            flops=3 * 2 * n * HALF * p, bytes_accessed=16 * 2**20, transcendentals=0
        ),
    )(*args)


def fit_kernel(p, f, out):
    out[0] = nt(p[...], f[0]).astype(jnp.bfloat16)


def fit(points, fitting, start, count):
    n, k = points.shape
    m = fitting.shape[1]
    return pl.pallas_call(
        fit_kernel,
        grid=(count,),
        in_specs=[
            pl.BlockSpec((n, k), lambda s: (0, 0)),
            pl.BlockSpec((1, m, k), lambda s: (s + start, 0, 0)),
        ],
        out_specs=pl.BlockSpec((1, n, m), lambda s: (s, 0, 0)),
        out_shape=jax.ShapeDtypeStruct((count, n, m), jnp.bfloat16),
        compiler_params=pltpu.CompilerParams(vmem_limit_bytes=VMEM),
        cost_estimate=pl.CostEstimate(
            flops=6 * n * m * k * count, bytes_accessed=2 * count * m * k, transcendentals=0
        ),
    )(points, fitting)


def parts(blocks, axis, mine, hop):
    def pick(d):
        return lax.dynamic_index_in_dim(blocks, (mine + d) % SIDE, axis, keepdims=False)

    got = [send(pick(d).astype(jnp.bfloat16), hop(d)) for d in (1, 3, 2)]
    return [pick(0)] + got


def total(pieces):
    out = pieces[0].astype(jnp.float32)
    for piece in pieces[1:]:
        out = out + piece.astype(jnp.float32)
    return out


def per_device(slopes, valid, sensor_map, reconstructor, fitting):
    s_idx = lax.axis_index("sens")
    l_idx = lax.axis_index("layer")
    z, c = s_idx // 2, s_idx % 2
    y, x = l_idx // 4, l_idx % 4
    width = slopes.shape[1]
    width_p = reconstructor.shape[0]
    act = fitting.shape[0]

    everything = lax.all_gather(fitting, "sens", axis=0)

    masked = slopes * valid.astype(jnp.bfloat16)[None, :]
    first_rows, second_rows = masked[: CUTS[0]], masked[CUTS[0] :]
    pad = ((0, 0), (0, HALF + BWIDTH - width))
    a0 = [first_rows[:, :HALF]]
    a1 = [second_rows[:, :HALF]]
    b1 = [jnp.pad(second_rows[:, HALF:], pad)]
    a0.append(ring_x(a0[-1]))
    b1.append(ring_y(b1[-1]))

    group = sensor_map * 2 + (lax.iota(jnp.int32, width) + s_idx * width) % 2
    lane = lax.iota(jnp.int32, 128)
    label = jnp.where(lane < INSIDE, -1, (lane - INSIDE) % 12)
    label = jnp.where(lane < INSIDE + 2 * SPAN, label, -1)
    member = ((group[None, :] == label[:, None]) & (valid[None, :] == 1)).astype(jnp.bfloat16)
    counted = jnp.concatenate([masked, jnp.ones((8, width), jnp.bfloat16)], axis=0)
    stats = nt(counted, member)
    stats, a0[1], b1[1] = after(stats, a0[1], b1[1])

    a0.append(ring_x(a0[-1]))
    b1.append(ring_y(b1[-1]))
    stats = stats + swap_core(stats)
    a0.append(ring_x(a0[-1]))
    b1.append(ring_y(b1[-1]))
    others = [send(stats, hop_z(d)) for d in (1, 3, 2)]
    stats = (stats + others[2]) + (others[0] + others[1])
    means = stats[:ROWS] / jnp.maximum(stats[ROWS : ROWS + 1], 1.0)
    high = lax.reduce_precision(means, 8, 7)
    low = means - high
    order = (lane - INSIDE) % SPAN < 12
    split = jnp.where(order[None, :], high, low)
    here = (lane >= INSIDE) & (lane < INSIDE + SPAN)
    there = (lane >= INSIDE + SPAN) & (lane < INSIDE + 2 * SPAN)
    rows = jnp.where(here[None, :], split[: CUTS[0]], 0.0)
    rows = rows + jnp.where(there[None, :], split[CUTS[0] :], 0.0)
    b0 = [jnp.pad(first_rows[:, HALF:], pad)]
    b0[0] = b0[0] + jnp.pad(rows.astype(jnp.bfloat16), ((0, 0), (EDGE, 0)))

    rw = -nt(reconstructor, member)
    rw0 = jnp.where(here[None, :], rw, 0.0)
    rw1 = jnp.where(there[None, :], rw, 0.0)

    block_a0 = [jnp.concatenate(a0, axis=0)]
    block_a0.append(ring_y(block_a0[-1]))
    for _ in range(3):
        b0.append(ring_y(b0[-1]))
        a1.append(ring_x(a1[-1]))
    block_b0 = [jnp.concatenate(b0, axis=0)]
    for _ in range(2):
        block_a0.append(ring_y(block_a0[-1]))
    for _ in range(3):
        block_b0.append(ring_x(block_b0[-1]))

    block_a1 = [jnp.concatenate(a1, axis=0)]
    block_b1 = [jnp.concatenate(b1, axis=0)]
    block_a1.append(ring_y(block_a1[-1]))
    block_b1.append(ring_x(block_b1[-1]))

    acc = matmul_a(CUTS[0], block_a0, reconstructor)
    acc, block_a1[1] = after(acc, block_a1[1])
    block_a1.append(ring_y(block_a1[-1]))
    own, other, tail = matmul_b(CUTS[0], 0, block_b0, reconstructor, rw0, acc, None)
    own, other, block_b1[1] = after(own, other, block_b1[1])
    block_b1.append(ring_x(block_b1[-1]))

    def layers_of(own, other, size):
        got = own + swap_core(other).astype(jnp.float32)
        got = got.reshape(SIDE, 2, size, width_p)
        return got

    layers0 = layers_of(own, other, CUTS[0])
    layers0, block_a1[2] = after(layers0, block_a1[2])
    block_a1.append(ring_y(block_a1[-1]))
    block_b1.append(ring_x(block_b1[-1]))
    points0 = total(parts(layers0, 0, z, hop_z)).astype(jnp.bfloat16)

    acc = matmul_a(CUTS[1], block_a1, reconstructor)
    own, other = matmul_b(CUTS[1], 1, block_b1, reconstructor, rw1, acc, tail)
    layers1 = layers_of(own, other, CUTS[1])
    points1 = total(parts(layers1, 0, z, hop_z)).astype(jnp.bfloat16)
    points = jnp.concatenate([points0, points1], axis=1)

    rows = points.reshape(SIDE, SIDE, 8, width_p)
    rows = jnp.where(c == 0, rows, jnp.swapaxes(rows, 0, 1)).reshape(2 * ROWS, width_p)
    one = jnp.where(c == 0, y, x)
    two = jnp.where(c == 0, x, y)
    half_a = fit(rows, everything, 0, 4).reshape(4, SIDE, 4 * 8, act)
    part_a = parts(half_a, 1, one, hop_one)
    half_b = fit(rows, everything, 4, 4).reshape(4, SIDE, 4 * 8, act)
    part_b = parts(half_b, 1, one, hop_one)
    both = jnp.concatenate([total(part_a), total(part_b)], axis=0)
    done = total(parts(both.reshape(8, SIDE, 8, act), 1, two, hop_two))
    return jnp.moveaxis(done, 0, 1).reshape(8, 8 * act)


def solution(mesh):
    placed = (P("layer", "sens"), P("sens"), P("sens"), P("layer", "sens"), P("sens", "layer"))
    return jax.shard_map(
        per_device,
        mesh=mesh,
        in_specs=placed,
        out_specs=P(("sens", "layer"), None),
        check_vma=False,
    )
```

```python
import functools

import jax
import jax.numpy as jnp
from jax import lax
from jax.experimental import pallas as pl
from jax.experimental.pallas import tpu as pltpu
from jax.sharding import PartitionSpec as P

SENSORS = 6
AXES = ("sens", "layer")
SIDE = 4
ROWS = 64
HALF = 4096
QUARTER = 2048
BWIDTH = 3968
EDGE = BWIDTH - 128
INSIDE = 14
SPAN = 24
PBLOCK = 256
VMEM = 52 * 2**20


def moved(fn):
    pairs = []
    for z in range(4):
        for c in range(2):
            for y in range(4):
                for x in range(4):
                    z2, c2, y2, x2 = fn(z, c, y, x)
                    pairs.append(
                        ((z * 2 + c) * 16 + y * 4 + x,
                         ((z2 % 4) * 2 + c2 % 2) * 16 + (y2 % 4) * 4 + x2 % 4)
                    )
    return pairs


def send(x, fn):
    return lax.ppermute(x, AXES, moved(fn))


def swap_core(v):
    return send(v, lambda z, c, y, x: (z, c + 1, y, x))


def right(v):
    return send(v, lambda z, c, y, x: (z, c, y, x + 1))


def left(v):
    return send(v, lambda z, c, y, x: (z, c, y, x - 1))


def up(v):
    return send(v, lambda z, c, y, x: (z, c, y + 1, x))


def down(v):
    return send(v, lambda z, c, y, x: (z, c, y - 1, x))


def hop_z(d):
    return lambda z, c, y, x: (z + d, c, y, x)


def hop_one(d):
    return lambda z, c, y, x: (z, c, y + d * (1 - c), x + d * c)


def hop_two(d):
    return lambda z, c, y, x: (z, c, y + d * c, x + d * (1 - c))


def home(z, c, y, x):
    layer = y * 4 + x
    sens, layer = layer // 2, 8 * (layer % 2) + z * 2 + c
    return (sens // 2, sens % 2, layer // 4, layer % 4)


def after(value, *others):
    return lax.optimization_barrier((value, *others))


def nt(a, b, **kw):
    return lax.dot_general(
        a, b, (((1,), (1,)), ((), ())), preferred_element_type=jnp.float32, **kw
    )


def reconstruct_kernel(pieces, count, *refs):
    arrays = refs[:count]
    core, ra, rb, rw, own, other, held, sems = refs[count:]

    @pl.when(pl.program_id(0) == 0)
    def _():
        copies = []
        for i, (a, row, rows, to_row, to_col) in enumerate(pieces):
            width = arrays[a].shape[1]
            copies.append(
                pltpu.make_async_copy(
                    arrays[a].at[pl.ds(row, rows)],
                    held.at[pl.ds(to_row, rows), pl.ds(to_col, width)],
                    sems.at[i],
                )
            )
        for copy in copies:
            copy.start()
        for copy in copies:
            copy.wait()

    lane = lax.broadcasted_iota(jnp.int32, (ra.shape[0], 128), 1)
    edge = jnp.where(
        lane < INSIDE, rb[:, EDGE:BWIDTH].astype(jnp.float32), rw[:, :128].astype(jnp.float32)
    ).astype(jnp.bfloat16)
    tail = held[:, HALF + EDGE :]
    val = nt(held[:, :HALF], ra[...]) + nt(held[:, HALF : HALF + EDGE], rb[:, :EDGE])
    val = val + nt(tail, edge) + nt(tail, rw[:, 128:])
    n = val.shape[0]
    pairs = val.reshape(n // 16, 2, 8, val.shape[1])
    first = pairs[:, 0].reshape(n // 2, val.shape[1])
    second = pairs[:, 1].reshape(n // 2, val.shape[1])
    swapped = core[0] == 1
    own[...] = jnp.where(swapped, second, first)
    other[...] = jnp.where(swapped, first, second).astype(jnp.bfloat16)


def reconstruct(sources, core, r, rw):
    arrays, pieces = [], []
    for k, source in enumerate(sources):
        for array, row, col in source:
            found = [i for i, a in enumerate(arrays) if a is array]
            if not found:
                arrays.append(array)
                found = [len(arrays) - 1]
            pieces.append((found[0], row, ROWS, k * ROWS, col))
    n = ROWS * len(sources)
    p = r.shape[0]
    half = pl.BlockSpec((n // 2, PBLOCK), lambda j: (0, j))
    return pl.pallas_call(
        functools.partial(reconstruct_kernel, tuple(pieces), len(arrays)),
        grid=(pl.cdiv(p, PBLOCK),),
        in_specs=[pl.BlockSpec(memory_space=pl.ANY)] * len(arrays)
        + [
            pl.BlockSpec(memory_space=pltpu.SMEM),
            pl.BlockSpec((PBLOCK, HALF), lambda j: (j, 0)),
            pl.BlockSpec((PBLOCK, HALF), lambda j: (j, 1)),
            pl.BlockSpec((PBLOCK, 256), lambda j: (j, 0)),
        ],
        out_specs=[half, half],
        out_shape=[
            jax.ShapeDtypeStruct((n // 2, p), jnp.float32),
            jax.ShapeDtypeStruct((n // 2, p), jnp.bfloat16),
        ],
        scratch_shapes=[
            pltpu.VMEM((n, HALF + BWIDTH), jnp.bfloat16),
            pltpu.SemaphoreType.DMA((len(pieces),)),
        ],
        compiler_params=pltpu.CompilerParams(vmem_limit_bytes=VMEM),
        cost_estimate=pl.CostEstimate(
            flops=4 * n * 8000 * p, bytes_accessed=24 * 2**20, transcendentals=0
        ),
    )(*arrays, core, r, r, rw)


def fit_kernel(p, f, out):
    out[0] = nt(p[...], f[0]).astype(jnp.bfloat16)


def fit(points, fitting, start, count):
    n, k = points.shape
    m = fitting.shape[1]
    return pl.pallas_call(
        fit_kernel,
        grid=(count,),
        in_specs=[
            pl.BlockSpec((n, k), lambda s: (0, 0)),
            pl.BlockSpec((1, m, k), lambda s: (s + start, 0, 0)),
        ],
        out_specs=pl.BlockSpec((1, n, m), lambda s: (s, 0, 0)),
        out_shape=jax.ShapeDtypeStruct((count, n, m), jnp.bfloat16),
        compiler_params=pltpu.CompilerParams(vmem_limit_bytes=VMEM),
        cost_estimate=pl.CostEstimate(
            flops=6 * n * m * k * count, bytes_accessed=2 * count * m * k, transcendentals=0
        ),
    )(points, fitting)


def sums_by_z(own, other, z):
    got = own + swap_core(other).astype(jnp.float32)
    got = got.reshape(-1, SIDE, 8, own.shape[1])

    def pick(d):
        return lax.dynamic_index_in_dim(got, (z + d) % SIDE, 1, keepdims=False)

    pieces = [pick(0)] + [send(pick(d).astype(jnp.bfloat16), hop_z(d)) for d in (1, 3, 2)]
    return total(pieces).astype(jnp.bfloat16)


def owned(blocks, hop):
    pieces = [blocks[:, 0]]
    pieces += [send(blocks[:, d].astype(jnp.bfloat16), hop(d)) for d in (1, 3, 2)]
    return pieces


def total(pieces):
    out = pieces[0].astype(jnp.float32)
    for piece in pieces[1:]:
        out = out + piece.astype(jnp.float32)
    return out


def per_device(slopes, valid, sensor_map, reconstructor, fitting):
    s_idx = lax.axis_index("sens")
    z, c = s_idx // 2, s_idx % 2
    width = slopes.shape[1]
    width_p = reconstructor.shape[0]
    act = fitting.shape[0]
    core = jnp.full((1,), c, jnp.int32)

    everything = lax.all_gather(fitting, "sens", axis=0)

    live = valid.astype(jnp.bfloat16)[None, :]
    a = {(0, 0): slopes[:, :HALF] * live[:, :HALF]}
    own_a = a[0, 0]
    from_left, from_right = right(own_a), left(own_a)
    from_down, from_up = up(own_a), down(own_a)

    masked = slopes * live
    group = sensor_map * 2 + (lax.iota(jnp.int32, width) + s_idx * width) % 2
    lane = lax.iota(jnp.int32, 128)
    inside = (lane >= INSIDE) & (lane < INSIDE + SPAN)
    label = jnp.where(inside, (lane - INSIDE) % 12, -1)
    member = ((group[None, :] == label[:, None]) & (valid[None, :] == 1)).astype(jnp.bfloat16)
    counted = jnp.concatenate([masked, jnp.ones((8, width), jnp.bfloat16)], axis=0)
    stats = nt(counted, member)
    stats = stats + swap_core(stats)
    others = [send(stats, hop_z(d)) for d in (1, 3, 2)]
    stats = (stats + others[2]) + (others[0] + others[1])
    means = stats[:ROWS] / jnp.maximum(stats[ROWS : ROWS + 1], 1.0)
    high = lax.reduce_precision(means, 8, 7)
    rows = jnp.where((lane < INSIDE + 12)[None, :], high, means - high)
    rows = jnp.where(inside[None, :], rows, 0.0).astype(jnp.bfloat16)
    own_b = jnp.pad(masked[:, HALF:], ((0, 0), (0, HALF + BWIDTH - width)))
    own_b = own_b + jnp.pad(rows, ((0, 0), (EDGE, 0)))

    b_left, b_right = right(own_b), left(own_b)
    b_down, b_up = up(own_b), down(own_b)

    rw = -nt(reconstructor, member)
    rw_high = lax.reduce_precision(rw, 8, 7)
    rw = jnp.concatenate([rw_high, rw - rw_high], axis=1).astype(jnp.bfloat16)

    pair = jnp.concatenate([from_left, from_right], axis=0)
    a_down, a_up = up(pair), down(pair)
    far_x_a = right(from_left)
    far_y_a = up(from_down)
    pair_b = jnp.concatenate([b_down, b_up], axis=0)
    bx_left, bx_right = right(pair_b), left(pair_b)
    far_x_b = left(b_right)
    far_y_b = down(b_up)

    def whole(array_a, array_b, row_a=0, row_b=0):
        return [(array_a, row_a, 0), (array_b, row_b, HALF)]

    own0, other0 = reconstruct(
        [
            whole(own_a, own_b),
            whole(from_left, b_left),
            whole(from_right, b_right),
            whole(from_down, b_down),
            whole(from_up, b_up),
        ],
        core, reconstructor, rw,
    )

    own0, other0, far_x_a, far_y_b = after(own0, other0, far_x_a, far_y_b)
    c_down, c_up = up(far_x_a), down(far_x_a)
    c_low = up(a_down[:, :QUARTER])
    c_high = down(a_up[:, QUARTER:])
    d_left, d_right = right(far_y_b), left(far_y_b)
    d_low = right(bx_left[:, :QUARTER])
    d_high = left(bx_right[:, QUARTER:])

    own1, other1 = reconstruct(
        [
            whole(a_down, bx_left, 0, 0),
            whole(a_down, bx_right, ROWS, 0),
            whole(a_up, bx_left, 0, ROWS),
            whole(a_up, bx_right, ROWS, ROWS),
            whole(far_x_a, far_x_b),
            whole(far_y_a, far_y_b),
        ],
        core, reconstructor, rw,
    )

    own1, other1, c_down, c_up, d_left, d_right = after(own1, other1, c_down, c_up, d_left, d_right)
    e_a_low = up(c_down[:, :QUARTER])
    e_a_high = down(c_up[:, QUARTER:])
    e_b_low = right(d_left[:, :QUARTER])
    e_b_high = left(d_right[:, QUARTER:])

    near = sums_by_z(
        jnp.concatenate([own0, own1], axis=0), jnp.concatenate([other0, other1], axis=0), z
    )
    near, e_a_low = after(near, e_a_low)

    own2, other2 = reconstruct(
        [
            [(c_down, 0, 0), (d_low, 0, HALF), (d_high, 0, HALF + QUARTER)],
            [(c_up, 0, 0), (d_low, ROWS, HALF), (d_high, ROWS, HALF + QUARTER)],
            [(c_low, 0, 0), (c_high, 0, QUARTER), (d_left, 0, HALF)],
            [(c_low, ROWS, 0), (c_high, ROWS, QUARTER), (d_right, 0, HALF)],
            [(e_a_low, 0, 0), (e_a_high, 0, QUARTER), (e_b_low, 0, HALF),
             (e_b_high, 0, HALF + QUARTER)],
        ],
        core, reconstructor, rw,
    )
    far = sums_by_z(own2, other2, z)

    names = [
        (0, 0), (0, 3), (0, 1), (3, 0), (1, 0),
        (3, 3), (3, 1), (1, 3), (1, 1), (0, 2), (2, 0),
        (3, 2), (1, 2), (2, 3), (2, 1), (2, 2),
    ]
    points = jnp.concatenate([near, far], axis=0)
    y_first = jnp.stack([points[names.index((i, j))] for i in range(4) for j in range(4)])
    x_first = jnp.stack([points[names.index((i, j))] for j in range(4) for i in range(4)])
    rows = jnp.where(c == 0, y_first, x_first).reshape(16 * 8, width_p)
    half_a = owned(fit(rows, everything, 0, 4).reshape(4, SIDE, SIDE * 8, act), hop_one)
    half_b = owned(fit(rows, everything, 4, 4).reshape(4, SIDE, SIDE * 8, act), hop_one)
    both = jnp.concatenate([total(half_a), total(half_b)], axis=0)
    done = total(owned(both.reshape(8, SIDE, 8, act), hop_two)).astype(jnp.bfloat16)
    done = jnp.moveaxis(done, 0, 1).reshape(8, 8 * act)
    return send(done, home).astype(jnp.float32)


def solution(mesh):
    placed = (P("layer", "sens"), P("sens"), P("sens"), P("layer", "sens"), P("sens", "layer"))
    return jax.shard_map(
        per_device,
        mesh=mesh,
        in_specs=placed,
        out_specs=P(("sens", "layer"), None),
        check_vma=False,
    )
```

```python
import functools

import jax
import jax.numpy as jnp
from jax import lax
from jax.experimental import pallas as pl
from jax.experimental.pallas import tpu as pltpu
from jax.sharding import PartitionSpec as P

SENSORS = 6
AXES = ("sens", "layer")
SIDE = 4
ROWS = 64
HALF = 4096
BWIDTH = 3968
EDGE = BWIDTH - 128
WIDE = HALF + BWIDTH
INSIDE = 14
PBLOCK = 256
VMEM = 52 * 2**20


def moved(fn):
    pairs = []
    for z in range(4):
        for c in range(2):
            for y in range(4):
                for x in range(4):
                    z2, c2, y2, x2 = fn(z, c, y, x)
                    pairs.append(
                        ((z * 2 + c) * 16 + y * 4 + x,
                         ((z2 % 4) * 2 + c2 % 2) * 16 + (y2 % 4) * 4 + x2 % 4)
                    )
    return pairs


def send(x, fn):
    return lax.ppermute(x, AXES, moved(fn))


def swap_core(v):
    return send(v, lambda z, c, y, x: (z, c + 1, y, x))


def right(v):
    return send(v, lambda z, c, y, x: (z, c, y, x + 1))


def left(v):
    return send(v, lambda z, c, y, x: (z, c, y, x - 1))


def up(v):
    return send(v, lambda z, c, y, x: (z, c, y + 1, x))


def down(v):
    return send(v, lambda z, c, y, x: (z, c, y - 1, x))


def hop_z(d):
    return lambda z, c, y, x: (z + d, c, y, x)


def hop_one(d):
    return lambda z, c, y, x: (z, c, y + d * (1 - c), x + d * c)


def hop_two(d):
    return lambda z, c, y, x: (z, c, y + d * c, x + d * (1 - c))


def home(z, c, y, x):
    layer = y * 4 + x
    sens, layer = layer // 2, 8 * (layer % 2) + z * 2 + c
    return (sens // 2, sens % 2, layer // 4, layer % 4)


def after(value, *others):
    return lax.optimization_barrier((value, *others))


def nt(a, b, **kw):
    return lax.dot_general(
        a, b, (((1,), (1,)), ((), ())), preferred_element_type=jnp.float32, **kw
    )


def reconstruct_kernel(pieces, places, count, *refs):
    arrays = refs[:count]
    position, means, ra, rb, rw, own, other, held, offsets, sems = refs[count:]

    @pl.when(pl.program_id(0) == 0)
    def _():
        copies = []
        for i, (a, row, rows, cols, to_row, to_col) in enumerate(pieces):
            copies.append(
                pltpu.make_async_copy(
                    arrays[a].at[pl.ds(row, rows), pl.ds(0, cols)],
                    held.at[pl.ds(to_row, rows), pl.ds(to_col, cols)],
                    sems.at[i],
                )
            )
        for k, (ry, rx) in enumerate(places):
            source = lax.rem(position[1] + ry, SIDE) * SIDE + lax.rem(position[2] + rx, SIDE)
            copies.append(
                pltpu.make_async_copy(
                    means.at[source],
                    offsets.at[pl.ds(k * ROWS, ROWS)],
                    sems.at[len(pieces) + k],
                )
            )
        for copy in copies:
            copy.start()
        for copy in copies:
            copy.wait()

    lane = lax.broadcasted_iota(jnp.int32, (ra.shape[0], 128), 1)
    edge = rb[:, EDGE:BWIDTH].astype(jnp.float32)
    edge = jnp.where(lane < INSIDE, edge, 0.0).astype(jnp.bfloat16)
    val = nt(held[:, :HALF], ra[...]) + nt(held[:, HALF : HALF + EDGE], rb[:, :EDGE])
    val = val + nt(held[:, HALF + EDGE :], edge) + nt(offsets[...], rw[...])
    n = val.shape[0]
    pairs = val.reshape(n // 16, 2, 8, val.shape[1])
    first = pairs[:, 0].reshape(n // 2, val.shape[1])
    second = pairs[:, 1].reshape(n // 2, val.shape[1])
    swapped = position[0] == 1
    own[...] = jnp.where(swapped, second, first)
    other[...] = jnp.where(swapped, first, second).astype(jnp.bfloat16)


def reconstruct(sources, position, means, r, rw):
    arrays, pieces = [], []
    for k, source in enumerate(sources.values()):
        for array, row, rows, cols, to_row, to_col in source:
            found = [i for i, a in enumerate(arrays) if a is array]
            if not found:
                arrays.append(array)
                found = [len(arrays) - 1]
            pieces.append((found[0], row, rows, cols, k * ROWS + to_row, to_col))
    n = ROWS * len(sources)
    p = r.shape[0]
    half = pl.BlockSpec((n // 2, PBLOCK), lambda j: (0, j))
    return pl.pallas_call(
        functools.partial(reconstruct_kernel, tuple(pieces), tuple(sources), len(arrays)),
        grid=(pl.cdiv(p, PBLOCK),),
        in_specs=[pl.BlockSpec(memory_space=pl.ANY)] * len(arrays)
        + [
            pl.BlockSpec(memory_space=pltpu.SMEM),
            pl.BlockSpec(memory_space=pl.ANY),
            pl.BlockSpec((PBLOCK, HALF), lambda j: (j, 0)),
            pl.BlockSpec((PBLOCK, HALF), lambda j: (j, 1)),
            pl.BlockSpec((PBLOCK, 128), lambda j: (j, 0)),
        ],
        out_specs=[half, half],
        out_shape=[
            jax.ShapeDtypeStruct((n // 2, p), jnp.float32),
            jax.ShapeDtypeStruct((n // 2, p), jnp.bfloat16),
        ],
        scratch_shapes=[
            pltpu.VMEM((n, WIDE), jnp.bfloat16),
            pltpu.VMEM((n, 128), jnp.bfloat16),
            pltpu.SemaphoreType.DMA((len(pieces) + len(sources),)),
        ],
        compiler_params=pltpu.CompilerParams(vmem_limit_bytes=VMEM),
        cost_estimate=pl.CostEstimate(flops=0, bytes_accessed=0, transcendentals=0),
    )(*arrays, position, means, r, r, rw)


def fit_kernel(p, f, out):
    out[0] = nt(p[...], f[0]).astype(jnp.bfloat16)


def fit(points, fitting, start, count):
    n, k = points.shape
    m = fitting.shape[1]
    return pl.pallas_call(
        fit_kernel,
        grid=(count,),
        in_specs=[
            pl.BlockSpec((n, k), lambda s: (0, 0)),
            pl.BlockSpec((1, m, k), lambda s: (s + start, 0, 0)),
        ],
        out_specs=pl.BlockSpec((1, n, m), lambda s: (s, 0, 0)),
        out_shape=jax.ShapeDtypeStruct((count, n, m), jnp.bfloat16),
        compiler_params=pltpu.CompilerParams(vmem_limit_bytes=VMEM),
        cost_estimate=pl.CostEstimate(
            flops=0, bytes_accessed=0, transcendentals=0
        ),
    )(points, fitting)


def picks_by_z(own, other, z):
    got = own + swap_core(other).astype(jnp.float32)
    got = got.reshape(-1, SIDE, 8, own.shape[1])

    def pick(d):
        return lax.dynamic_index_in_dim(got, (z + d) % SIDE, 1, keepdims=False)

    return [pick(0)] + [pick(d).astype(jnp.bfloat16) for d in (1, 3, 2)]


def sums_by_z(picked):
    pieces = picked[:1] + [send(v, hop_z(d)) for v, d in zip(picked[1:], (1, 3, 2))]
    return total(pieces).astype(jnp.bfloat16)


def owned(blocks, hop):
    pieces = [blocks[:, 0]]
    pieces += [send(blocks[:, d].astype(jnp.bfloat16), hop(d)) for d in (1, 3, 2)]
    return pieces


def total(pieces):
    out = pieces[0].astype(jnp.float32)
    for piece in pieces[1:]:
        out = out + piece.astype(jnp.float32)
    return out


def together(*pieces):
    return jnp.concatenate(
        [jnp.pad(p, ((0, 0), (0, HALF - p.shape[1]))) for p in pieces], axis=0
    )


def per_device(slopes, valid, sensor_map, reconstructor, fitting):
    s_idx = lax.axis_index("sens")
    l_idx = lax.axis_index("layer")
    z, c = s_idx // 2, s_idx % 2
    width = slopes.shape[1]
    width_p = reconstructor.shape[0]
    act = fitting.shape[0]
    position = jnp.stack([c, l_idx // SIDE, l_idx % SIDE]).astype(jnp.int32)

    everything = lax.all_gather(fitting, "sens", axis=0)

    live = valid.astype(jnp.bfloat16)[None, :]
    mine = jnp.pad(slopes * live, ((0, 0), (0, WIDE - width)))

    got_l, got_r = right(mine), left(mine)
    got_d, got_u = up(mine), down(mine)

    group = sensor_map * 2 + (lax.iota(jnp.int32, width) + s_idx * width) % 2
    lane = lax.iota(jnp.int32, 128)
    label = jnp.where(lane < 36, lane % 12, -1)
    member = ((group[None, :] == label[:, None]) & (valid[None, :] == 1)).astype(jnp.bfloat16)
    counted = jnp.concatenate([mine[:, :width], jnp.ones((8, width), jnp.bfloat16)], axis=0)
    stats = nt(counted, member)
    stats = jnp.broadcast_to(stats[None], (8, *stats.shape))
    stats = jnp.sum(lax.all_to_all(stats, "sens", 0, 0, tiled=True), axis=0)
    means = stats[:ROWS] / jnp.maximum(stats[ROWS : ROWS + 1], 1.0)
    high = lax.reduce_precision(means, 8, 7)
    low = (lane >= 12) & (lane < 24)
    means = jnp.where(low[None, :], means - high, high).astype(jnp.bfloat16)
    means = lax.all_gather(means, "layer", axis=0)

    send_u = together(got_l[:, :HALF], got_r[:, :HALF], got_d[:, :HALF])
    send_d = together(got_l[:, :HALF], got_r[:, :HALF], got_u[:, HALF:])
    send_r = together(got_d[:, HALF:], got_u[:, HALF:], got_l[:, :HALF])
    send_l = together(got_d[:, HALF:], got_u[:, HALF:], got_r[:, HALF:])
    member, send_u, send_d, send_r, send_l = after(member, send_u, send_d, send_r, send_l)
    one_d, one_u = up(send_u), down(send_d)
    one_l, one_r = right(send_r), left(send_l)
    rw = -nt(reconstructor, member)
    rw_high = lax.reduce_precision(rw, 8, 7)
    last = (lane >= 24) & (lane < 36)
    rw = jnp.where(last[None, :], rw - rw_high, rw_high).astype(jnp.bfloat16)

    def all_of(array):
        return [(array, 0, ROWS, WIDE, 0, 0)]

    def halves(array_a, index_a, array_b, index_b):
        return [
            (array_a, index_a * ROWS, ROWS, HALF, 0, 0),
            (array_b, index_b * ROWS, ROWS, BWIDTH, 0, HALF),
        ]

    own0, other0 = reconstruct(
        {
            (0, 0): all_of(mine),
            (0, 3): all_of(got_l),
            (0, 1): all_of(got_r),
            (3, 0): all_of(got_d),
            (1, 0): all_of(got_u),
        },
        position, means, reconstructor, rw,
    )

    own0, other0, one_d, one_u, one_l, one_r = after(own0, other0, one_d, one_u, one_l, one_r)
    far_x_a, far_x_b = one_l[2 * ROWS :], one_r[2 * ROWS :]
    far_y_a, far_y_b = one_d[2 * ROWS :], one_u[2 * ROWS :]
    two_d = together(far_x_a, one_d[:ROWS])
    two_u = together(far_x_a, one_u[ROWS : 2 * ROWS])
    two_l = together(far_y_b, one_l[:ROWS])
    two_r = together(far_y_b, one_r[ROWS : 2 * ROWS])
    two_d, two_u, two_l, two_r = after(two_d, two_u, two_l, two_r)
    get_d, get_u = up(two_d), down(two_u)
    get_l, get_r = right(two_l), left(two_r)

    own1, other1 = reconstruct(
        {
            (3, 3): halves(one_d, 0, one_l, 0),
            (3, 1): halves(one_d, 1, one_r, 0),
            (1, 3): halves(one_u, 0, one_l, 1),
            (1, 1): halves(one_u, 1, one_r, 1),
            (0, 2): halves(one_l, 2, one_r, 2),
            (2, 0): halves(one_d, 2, one_u, 2),
        },
        position, means, reconstructor, rw,
    )

    own1, other1, get_d, get_u, get_l, get_r = after(own1, other1, get_d, get_u, get_l, get_r)
    half = ROWS // 2
    end_d, end_u = up(get_d[:half]), down(get_u[half:ROWS])
    end_l, end_r = right(get_l[:half]), left(get_r[half:ROWS])

    picked = picks_by_z(
        jnp.concatenate([own0, own1], axis=0), jnp.concatenate([other0, other1], axis=0), z
    )
    *picked, end_d, end_u, end_l, end_r = after(*picked, end_d, end_u, end_l, end_r)
    near = sums_by_z(picked)

    own2, other2 = reconstruct(
        {
            (3, 2): halves(get_d, 0, get_l, 1),
            (1, 2): halves(get_u, 0, get_r, 1),
            (2, 3): halves(get_d, 1, get_l, 0),
            (2, 1): halves(get_u, 1, get_r, 0),
            (2, 2): [
                (end_d, 0, half, HALF, 0, 0),
                (end_u, 0, half, HALF, half, 0),
                (end_l, 0, half, BWIDTH, 0, HALF),
                (end_r, 0, half, BWIDTH, half, HALF),
            ],
        },
        position, means, reconstructor, rw,
    )
    far = sums_by_z(picks_by_z(own2, other2, z))

    names = [
        (0, 0), (0, 3), (0, 1), (3, 0), (1, 0),
        (3, 3), (3, 1), (1, 3), (1, 1), (0, 2), (2, 0),
        (3, 2), (1, 2), (2, 3), (2, 1), (2, 2),
    ]
    points = jnp.concatenate([near, far], axis=0)
    y_first = jnp.stack([points[names.index((i, j))] for i in range(4) for j in range(4)])
    x_first = jnp.stack([points[names.index((i, j))] for j in range(4) for i in range(4)])
    rows = jnp.where(c == 0, y_first, x_first).reshape(16 * 8, width_p)
    half_a = owned(fit(rows, everything, 0, 4).reshape(4, SIDE, SIDE * 8, act), hop_one)
    half_b = owned(fit(rows, everything, 4, 4).reshape(4, SIDE, SIDE * 8, act), hop_one)
    both = jnp.concatenate([total(half_a), total(half_b)], axis=0)
    done = total(owned(both.reshape(8, SIDE, 8, act), hop_two)).astype(jnp.bfloat16)
    done = jnp.moveaxis(done, 0, 1).reshape(8, 8 * act)
    return send(done, home).astype(jnp.float32)


def solution(mesh):
    placed = (P("layer", "sens"), P("sens"), P("sens"), P("layer", "sens"), P("sens", "layer"))
    return jax.shard_map(
        per_device,
        mesh=mesh,
        in_specs=placed,
        out_specs=P(("sens", "layer"), None),
        check_vma=False,
    )
```

```python
import functools

import jax
import jax.numpy as jnp
from jax import lax
from jax.experimental import pallas as pl
from jax.experimental.pallas import tpu as pltpu
from jax.sharding import PartitionSpec as P

SENSORS = 6
AXES = ("sens", "layer")
SIDE = 4
ROWS = 64
PART = 32
HALF = 4096
EDGE = 3840
MEANS = 3968
WIDE = 8064
INSIDE = 14
PBLOCK = 256
VMEM = 52 * 2**20


def moved(fn):
    pairs = []
    for z in range(4):
        for c in range(2):
            for y in range(4):
                for x in range(4):
                    z2, c2, y2, x2 = fn(z, c, y, x)
                    pairs.append(
                        ((z * 2 + c) * 16 + y * 4 + x,
                         ((z2 % 4) * 2 + c2 % 2) * 16 + (y2 % 4) * 4 + x2 % 4)
                    )
    return pairs


def send(x, fn):
    return lax.ppermute(x, AXES, moved(fn))


def swap_core(v):
    return send(v, lambda z, c, y, x: (z, c + 1, y, x))


def right(v):
    return send(v, lambda z, c, y, x: (z, c, y, x + 1))


def left(v):
    return send(v, lambda z, c, y, x: (z, c, y, x - 1))


def up(v):
    return send(v, lambda z, c, y, x: (z, c, y + 1, x))


def down(v):
    return send(v, lambda z, c, y, x: (z, c, y - 1, x))


def hop_z(d):
    return lambda z, c, y, x: (z + d, c, y, x)


def hop_one(d):
    return lambda z, c, y, x: (z, c, y + d * (1 - c), x + d * c)


def hop_two(d):
    return lambda z, c, y, x: (z, c, y + d * c, x + d * (1 - c))


def ring_z(v):
    return send(v, lambda z, c, y, x: (z + 1 - 2 * c, c, y, x))


def after(value, *others):
    return lax.optimization_barrier((value, *others))


def nt(a, b, **kw):
    return lax.dot_general(
        a, b, (((1,), (1,)), ((), ())), preferred_element_type=jnp.float32, **kw
    )


def reconstruct_kernel(pieces, count, index, *refs):
    arrays = refs[:count]
    if index == 0:
        position, ra, rb, rw, own, other, tail, held, sems = refs[count:]
    else:
        position, ra, rb, rw, tail, own, other, held, sems = refs[count:]

    def copies(side):
        out = []
        for i, (a, row, rows, ry, rx, inner, half) in enumerate(pieces):
            if half != side:
                continue
            if index == 0:
                y = lax.rem(position[1] + ry, SIDE)
                x = lax.rem(position[2] + rx, SIDE)
                to_row = pl.multiple_of((y * SIDE + x) * PART, PART) + inner
                source = arrays[a].at[pl.ds(row, rows)]
                width = HALF
            else:
                to_row = row
                width = HALF if half == 0 else WIDE - HALF
                source = arrays[a].at[pl.ds(row, rows), pl.ds(half * HALF, width)]
            target = held.at[pl.ds(to_row, rows), pl.ds(half * HALF, width)]
            out.append(pltpu.make_async_copy(source, target, sems.at[i]))
        return out

    @pl.when(pl.program_id(0) == 0)
    def _():
        for copy in copies(0) + copies(1):
            copy.start()
        for copy in copies(0):
            copy.wait()

    val = nt(held[:, :HALF], ra[...])

    @pl.when(pl.program_id(0) == 0)
    def _():
        for copy in copies(1):
            copy.wait()

    lane = lax.broadcasted_iota(jnp.int32, (ra.shape[0], 128), 1)
    edge = rb[:, EDGE:MEANS].astype(jnp.float32)
    edge = jnp.where(lane < INSIDE, edge, 0.0).astype(jnp.bfloat16)
    val = val + nt(held[:, HALF : HALF + EDGE], rb[:, :EDGE])
    val = val + nt(held[:, HALF + EDGE : HALF + MEANS], edge)
    if index == 0:
        means = held[:, HALF + MEANS :]
        tail[...] = means
    else:
        means = tail[...]
    val = val + nt(means, rw[...])
    n = val.shape[0]
    pairs = val.reshape(SIDE, 2, 2 * PART, val.shape[1])
    first = pairs[:, 0].reshape(n // 2, val.shape[1])
    second = pairs[:, 1].reshape(n // 2, val.shape[1])
    swapped = position[0] == 1
    own[...] = jnp.where(swapped, second, first)
    other[...] = jnp.where(swapped, first, second).astype(jnp.bfloat16)


def reconstruct(index, arrays, pieces, position, r, rw, tail=None):
    n = 16 * PART
    p = r.shape[0]
    half = pl.BlockSpec((n // 2, PBLOCK), lambda j: (0, j))
    whole = pl.BlockSpec((n, 128), lambda j: (0, 0))
    in_specs = [pl.BlockSpec(memory_space=pl.ANY)] * len(arrays) + [
        pl.BlockSpec(memory_space=pltpu.SMEM),
        pl.BlockSpec((PBLOCK, HALF), lambda j: (j, 0)),
        pl.BlockSpec((PBLOCK, HALF), lambda j: (j, 1)),
        pl.BlockSpec((PBLOCK, 128), lambda j: (j, index)),
    ]
    args = [*arrays, position, r, r, rw]
    out_specs = [half, half]
    out_shape = [
        jax.ShapeDtypeStruct((n // 2, p), jnp.float32),
        jax.ShapeDtypeStruct((n // 2, p), jnp.bfloat16),
    ]
    if index == 0:
        out_specs.append(whole)
        out_shape.append(jax.ShapeDtypeStruct((n, 128), jnp.bfloat16))
    else:
        in_specs.append(whole)
        args.append(tail)
    return pl.pallas_call(
        functools.partial(reconstruct_kernel, tuple(pieces), len(arrays), index),
        grid=(pl.cdiv(p, PBLOCK),),
        in_specs=in_specs,
        out_specs=out_specs,
        out_shape=out_shape,
        scratch_shapes=[
            pltpu.VMEM((n, 2 * HALF), jnp.bfloat16),
            pltpu.SemaphoreType.DMA((len(pieces),)),
        ],
        compiler_params=pltpu.CompilerParams(vmem_limit_bytes=VMEM),
        cost_estimate=pl.CostEstimate(flops=0, bytes_accessed=0, transcendentals=0),
    )(*args)


def fit_kernel(p, f0, f1, f2, f3, out, held, sems):
    sources = (f0, f1, f2, f3)
    copies = [
        pltpu.make_async_copy(f, held.at[i], sems.at[i]) for i, f in enumerate(sources)
    ]
    for copy in copies:
        copy.start()
    for i, copy in enumerate(copies):
        copy.wait()
        out[i] = nt(p[...], held[i]).astype(jnp.bfloat16)


def fit(points, blocks):
    n, k = points.shape
    m = blocks[0].shape[0]
    return pl.pallas_call(
        fit_kernel,
        in_specs=[pl.BlockSpec(memory_space=pltpu.VMEM)]
        + [pl.BlockSpec(memory_space=pl.ANY)] * 4,
        out_specs=pl.BlockSpec(memory_space=pltpu.VMEM),
        out_shape=jax.ShapeDtypeStruct((4, n, m), jnp.bfloat16),
        scratch_shapes=[
            pltpu.VMEM((4, m, k), jnp.bfloat16),
            pltpu.SemaphoreType.DMA((4,)),
        ],
        compiler_params=pltpu.CompilerParams(vmem_limit_bytes=VMEM),
        cost_estimate=pl.CostEstimate(flops=0, bytes_accessed=0, transcendentals=0),
    )(points, *blocks)


def picks_by_z(own, other, z):
    got = own + swap_core(other).astype(jnp.float32)
    got = got.reshape(SIDE, 2, PART, own.shape[1])

    def pick(d):
        return lax.dynamic_index_in_dim(got, (z + d) % SIDE, 0, keepdims=False)

    return [pick(0)] + [pick(d).astype(jnp.bfloat16) for d in (1, 3, 2)]


def sums_by_z(picked):
    pieces = picked[:1] + [send(v, hop_z(d)) for v, d in zip(picked[1:], (1, 3, 2))]
    return total(pieces).astype(jnp.bfloat16)


def owned(blocks, here, hop):
    def pick(d):
        return lax.dynamic_index_in_dim(blocks, (here + d) % SIDE, 1, keepdims=False)

    return [pick(0)] + [send(pick(d).astype(jnp.bfloat16), hop(d)) for d in (1, 3, 2)]


def total(pieces):
    out = pieces[0].astype(jnp.float32)
    for piece in pieces[1:]:
        out = out + piece.astype(jnp.float32)
    return out


def together(*pieces):
    return jnp.concatenate(pieces, axis=0)


def per_device(slopes, valid, sensor_map, reconstructor, fitting):
    s_idx = lax.axis_index("sens")
    l_idx = lax.axis_index("layer")
    z, c = s_idx // 2, s_idx % 2
    y, x = l_idx // SIDE, l_idx % SIDE
    width = slopes.shape[1]
    width_p = reconstructor.shape[0]
    act = fitting.shape[0]
    position = jnp.stack([c, y, x]).astype(jnp.int32)

    live = valid.astype(jnp.bfloat16)[None, :]
    masked = slopes * live
    late = lax.all_gather(
        jnp.pad(masked[PART:], ((0, 0), (0, WIDE - width))), "layer", axis=0, tiled=True
    )

    own_a = masked[:PART, :HALF]
    a_l, a_r = right(own_a), left(own_a)
    a_d, a_u = up(own_a), down(own_a)
    fits = [fitting, ring_z(fitting)]

    group = sensor_map * 2 + (lax.iota(jnp.int32, width) + s_idx * width) % 2
    lane = lax.iota(jnp.int32, 128)
    label = jnp.where(lane % 64 < 36, lane % 64 % 12, -1)
    member = ((group[None, :] == label[:, None]) & (valid[None, :] == 1)).astype(jnp.bfloat16)
    counted = jnp.concatenate([masked, jnp.ones((8, width), jnp.bfloat16)], axis=0)
    stats = nt(counted, member)
    stats = jnp.broadcast_to(stats[None], (8, *stats.shape))
    stats = jnp.sum(lax.all_to_all(stats, "sens", 0, 0, tiled=True), axis=0)
    means = stats[:ROWS] / jnp.maximum(stats[ROWS : ROWS + 1], 1.0)
    means = jnp.where((lane < 64)[None, :], means[:PART], means[PART:])
    high = lax.reduce_precision(means, 8, 7)
    low = (lane % 64 >= 12) & (lane % 64 < 24)
    means = jnp.where(low[None, :], means - high, high).astype(jnp.bfloat16)
    own_b = jnp.pad(masked[:PART, HALF:], ((0, 0), (0, 2 * HALF - width)))
    own_b = own_b + jnp.pad(means, ((0, 0), (MEANS, 0)))
    b_l, b_r = right(own_b), left(own_b)
    b_d, b_u = up(own_b), down(own_b)

    send_u = together(a_l, a_r, a_d)
    send_d = together(a_l, a_r, b_u)
    send_r = together(b_d, b_u, a_l)
    send_l = together(b_d, b_u, b_r)
    member, send_u, send_d, send_r, send_l, a_u, b_l, fits[1] = after(
        member, send_u, send_d, send_r, send_l, a_u, b_l, fits[1]
    )
    fits.append(ring_z(fits[-1]))
    one_d, one_u = up(send_u), down(send_d)
    one_l, one_r = right(send_r), left(send_l)
    rw = -nt(reconstructor, member)
    rw_high = lax.reduce_precision(rw, 8, 7)
    last = (lane % 64 >= 24) & (lane % 64 < 36)
    rw = jnp.where(last[None, :], rw - rw_high, rw_high)
    early = (lane < 64)[None, :]
    rw = jnp.concatenate([jnp.where(early, rw, 0.0), jnp.where(early, 0.0, rw)], axis=1)
    rw = rw.astype(jnp.bfloat16)

    fits[2], one_d, one_u, one_l, one_r, rw = after(fits[2], one_d, one_u, one_l, one_r, rw)
    fits.append(ring_z(fits[-1]))
    far_x_a, far_y_b = one_l[2 * PART :], one_u[2 * PART :]
    two_d = together(far_x_a, one_d[:PART])
    two_u = together(far_x_a, one_u[PART : 2 * PART])
    two_l = together(far_y_b, one_l[:PART])
    two_r = together(far_y_b, one_r[PART : 2 * PART])
    two_d, two_u, two_l, two_r = after(two_d, two_u, two_l, two_r)
    get_d, get_u = up(two_d), down(two_u)
    get_l, get_r = right(two_l), left(two_r)

    half = PART // 2
    ends = after(get_d[:half], get_u[half:PART], get_l[:half], get_r[half:PART])
    end_d, end_u = up(ends[0]), down(ends[1])
    end_l, end_r = right(ends[2]), left(ends[3])

    arrays = [own_a, own_b, a_l, b_l, a_r, b_r, a_d, b_d, a_u, b_u, one_d, one_u, one_l, one_r]
    arrays += [get_d, get_u, get_l, get_r, end_d, end_u, end_l, end_r]

    def piece(array, block, rows, ry, rx, inner, side):
        index = [i for i, a in enumerate(arrays) if a is array][0]
        return (index, block * rows, rows, ry, rx, inner, side)

    pieces = []
    for ry, rx, (array_a, block_a), (array_b, block_b) in (
        (0, 0, (own_a, 0), (own_b, 0)),
        (0, 3, (a_l, 0), (b_l, 0)),
        (0, 1, (a_r, 0), (b_r, 0)),
        (3, 0, (a_d, 0), (b_d, 0)),
        (1, 0, (a_u, 0), (b_u, 0)),
        (3, 3, (one_d, 0), (one_l, 0)),
        (3, 1, (one_d, 1), (one_r, 0)),
        (1, 3, (one_u, 0), (one_l, 1)),
        (1, 1, (one_u, 1), (one_r, 1)),
        (0, 2, (one_l, 2), (one_r, 2)),
        (2, 0, (one_d, 2), (one_u, 2)),
        (3, 2, (get_d, 0), (get_l, 1)),
        (1, 2, (get_u, 0), (get_r, 1)),
        (2, 3, (get_d, 1), (get_l, 0)),
        (2, 1, (get_u, 1), (get_r, 0)),
    ):
        pieces.append(piece(array_a, block_a, PART, ry, rx, 0, 0))
        pieces.append(piece(array_b, block_b, PART, ry, rx, 0, 1))
    pieces.append(piece(end_d, 0, half, 2, 2, 0, 0))
    pieces.append(piece(end_u, 0, half, 2, 2, half, 0))
    pieces.append(piece(end_l, 0, half, 2, 2, 0, 1))
    pieces.append(piece(end_r, 0, half, 2, 2, half, 1))
    own, other, tail = reconstruct(0, arrays, pieces, position, reconstructor, rw)
    own, other, *fits = after(own, other, *fits)
    picked = picks_by_z(own, other, z)
    swapped = [swap_core(f) for f in fits]
    swapped[0], swapped[1], *picked, late = after(swapped[0], swapped[1], *picked, late)
    near = sums_by_z(picked)

    own, other = reconstruct(
        1, [late], [(0, 0, 16 * PART, 0, 0, 0, side) for side in (0, 1)],
        position, reconstructor, rw, tail,
    )
    far = sums_by_z(picks_by_z(own, other, z))
    points = jnp.concatenate([near, far], axis=1)

    rows = points.reshape(SIDE, SIDE, 8, width_p)
    rows = jnp.where(c == 0, rows, jnp.swapaxes(rows, 0, 1)).reshape(2 * ROWS, width_p)
    one = jnp.where(c == 0, y, x)
    two = jnp.where(c == 0, x, y)
    half_a = owned(fit(rows, fits).reshape(4, SIDE, SIDE * 8, act), one, hop_one)
    half_b = owned(fit(rows, swapped).reshape(4, SIDE, SIDE * 8, act), one, hop_one)
    both = jnp.concatenate([total(half_a), total(half_b)], axis=0)
    done = total(owned(both.reshape(8, SIDE, 8, act), two, hop_two))

    sens = lax.iota(jnp.int32, 8)
    step = jnp.where(sens % 2 == 0, z - sens // 2, sens // 2 - z) % SIDE
    found = jnp.where(sens % 2 == c, 0, 4) + step
    done = jnp.take(done, found, axis=0)
    return jnp.moveaxis(done, 0, 1).reshape(8, 8 * act)


def solution(mesh):
    placed = (P("layer", "sens"), P("sens"), P("sens"), P("layer", "sens"), P("sens", "layer"))
    return jax.shard_map(
        per_device,
        mesh=mesh,
        in_specs=placed,
        out_specs=P(("sens", "layer"), None),
        check_vma=False,
    )
```

```python
import functools

import jax
import jax.numpy as jnp
from jax import lax
from jax.experimental import pallas as pl
from jax.experimental.pallas import tpu as pltpu
from jax.sharding import PartitionSpec as P

SENSORS = 6
AXES = ("sens", "layer")
SIDE = 4
ROWS = 64
PART = 16
LATE = ROWS - PART
LANES = 24
HALF = 4096
EDGE = 3840
MEANS = 3968
WIDE = 8064
INSIDE = 14
PBLOCK = 256
VMEM = 52 * 2**20


def moved(fn):
    pairs = []
    for z in range(4):
        for c in range(2):
            for y in range(4):
                for x in range(4):
                    z2, c2, y2, x2 = fn(z, c, y, x)
                    pairs.append(
                        ((z * 2 + c) * 16 + y * 4 + x,
                         ((z2 % 4) * 2 + c2 % 2) * 16 + (y2 % 4) * 4 + x2 % 4)
                    )
    return pairs


def send(x, fn):
    return lax.ppermute(x, AXES, moved(fn))


def swap_core(v):
    return send(v, lambda z, c, y, x: (z, c + 1, y, x))


def right(v):
    return send(v, lambda z, c, y, x: (z, c, y, x + 1))


def left(v):
    return send(v, lambda z, c, y, x: (z, c, y, x - 1))


def up(v):
    return send(v, lambda z, c, y, x: (z, c, y + 1, x))


def down(v):
    return send(v, lambda z, c, y, x: (z, c, y - 1, x))


def hop_z(d):
    return lambda z, c, y, x: (z + d, c, y, x)


def hop_one(d):
    return lambda z, c, y, x: (z, c, y + d * (1 - c), x + d * c)


def hop_two(d):
    return lambda z, c, y, x: (z, c, y + d * c, x + d * (1 - c))


def ring_z(v):
    return send(v, lambda z, c, y, x: (z + 1 - 2 * c, c, y, x))


def after(value, *others):
    return lax.optimization_barrier((value, *others))


def nt(a, b, **kw):
    return lax.dot_general(
        a, b, (((1,), (1,)), ((), ())), preferred_element_type=jnp.float32, **kw
    )


def reconstruct_kernel(pieces, count, index, *refs):
    arrays = refs[:count]
    if index == 0:
        position, ra, rb, rw, own, other, tail, held, sems = refs[count:]
    else:
        position, ra, rb, rw, tail, own, other, held, sems = refs[count:]

    def copies(side):
        out = []
        for i, (a, row, rows, ry, rx, half) in enumerate(pieces):
            if half != side:
                continue
            if index == 0:
                y = lax.rem(position[1] + ry, SIDE)
                x = lax.rem(position[2] + rx, SIDE)
                to_row = pl.multiple_of((y * SIDE + x) * PART, PART)
                source = arrays[a].at[pl.ds(row, rows)]
                width = HALF
            else:
                to_row = row
                width = HALF if half == 0 else WIDE - HALF
                source = arrays[a].at[pl.ds(row, rows), pl.ds(half * HALF, width)]
            target = held.at[pl.ds(to_row, rows), pl.ds(half * HALF, width)]
            out.append(pltpu.make_async_copy(source, target, sems.at[i]))
        return out

    @pl.when(pl.program_id(0) == 0)
    def _():
        for copy in copies(0) + copies(1):
            copy.start()
        for copy in copies(0):
            copy.wait()

    val = nt(held[:, :HALF], ra[...])

    @pl.when(pl.program_id(0) == 0)
    def _():
        for copy in copies(1):
            copy.wait()

    lane = lax.broadcasted_iota(jnp.int32, (ra.shape[0], 128), 1)
    edge = rb[:, EDGE:MEANS].astype(jnp.float32)
    edge = jnp.where(lane < INSIDE, edge, 0.0).astype(jnp.bfloat16)
    val = val + nt(held[:, HALF : HALF + EDGE], rb[:, :EDGE])
    val = val + nt(held[:, HALF + EDGE : HALF + MEANS], edge)
    high, low = rw[:, :128].astype(jnp.float32), rw[:, 128:].astype(jnp.float32)

    def moved_by(means, q):
        chosen = (lane >= q * LANES) & (lane < (q + 1) * LANES)
        one = jnp.where(chosen, high, 0.0).astype(jnp.bfloat16)
        two = jnp.where(chosen, low, 0.0).astype(jnp.bfloat16)
        return nt(means, one) + nt(means, two)

    n, p = val.shape
    if index == 0:
        means = held[:, HALF + MEANS :]
        tail[...] = means
        val = val + moved_by(means, 0)
    else:
        means = tail[...]
        shift = [moved_by(means, q).reshape(16, 1, PART, p) for q in range(1, ROWS // PART)]
        val = val.reshape(16, LATE // PART, PART, p) + jnp.concatenate(shift, axis=1)
    pairs = val.reshape(SIDE, 2, n // 8, p)
    first = pairs[:, 0].reshape(n // 2, p)
    second = pairs[:, 1].reshape(n // 2, p)
    swapped = position[0] == 1
    own[...] = jnp.where(swapped, second, first)
    other[...] = jnp.where(swapped, first, second).astype(jnp.bfloat16)


def reconstruct(index, arrays, pieces, position, r, rw, tail=None):
    n = 16 * (PART if index == 0 else LATE)
    p = r.shape[0]
    half = pl.BlockSpec((n // 2, PBLOCK), lambda j: (0, j))
    whole = pl.BlockSpec((16 * PART, 128), lambda j: (0, 0))
    in_specs = [pl.BlockSpec(memory_space=pl.ANY)] * len(arrays) + [
        pl.BlockSpec(memory_space=pltpu.SMEM),
        pl.BlockSpec((PBLOCK, HALF), lambda j: (j, 0)),
        pl.BlockSpec((PBLOCK, HALF), lambda j: (j, 1)),
        pl.BlockSpec((PBLOCK, 256), lambda j: (j, 0)),
    ]
    args = [*arrays, position, r, r, rw]
    out_specs = [half, half]
    out_shape = [
        jax.ShapeDtypeStruct((n // 2, p), jnp.float32),
        jax.ShapeDtypeStruct((n // 2, p), jnp.bfloat16),
    ]
    if index == 0:
        out_specs.append(whole)
        out_shape.append(jax.ShapeDtypeStruct((16 * PART, 128), jnp.bfloat16))
    else:
        in_specs.append(whole)
        args.append(tail)
    return pl.pallas_call(
        functools.partial(reconstruct_kernel, tuple(pieces), len(arrays), index),
        grid=(pl.cdiv(p, PBLOCK),),
        in_specs=in_specs,
        out_specs=out_specs,
        out_shape=out_shape,
        scratch_shapes=[
            pltpu.VMEM((n, 2 * HALF), jnp.bfloat16),
            pltpu.SemaphoreType.DMA((len(pieces),)),
        ],
        compiler_params=pltpu.CompilerParams(vmem_limit_bytes=VMEM),
        cost_estimate=pl.CostEstimate(flops=0, bytes_accessed=0, transcendentals=0),
    )(*args)


def fit_kernel(p, f0, f1, f2, f3, out, held, sems):
    sources = (f0, f1, f2, f3)
    copies = [
        pltpu.make_async_copy(f, held.at[i], sems.at[i]) for i, f in enumerate(sources)
    ]
    for copy in copies:
        copy.start()
    for i, copy in enumerate(copies):
        copy.wait()
        out[i] = nt(p[...], held[i]).astype(jnp.bfloat16)


def fit(points, blocks):
    n, k = points.shape
    m = blocks[0].shape[0]
    return pl.pallas_call(
        fit_kernel,
        in_specs=[pl.BlockSpec(memory_space=pltpu.VMEM)]
        + [pl.BlockSpec(memory_space=pl.ANY)] * 4,
        out_specs=pl.BlockSpec(memory_space=pltpu.VMEM),
        out_shape=jax.ShapeDtypeStruct((4, n, m), jnp.bfloat16),
        scratch_shapes=[
            pltpu.VMEM((4, m, k), jnp.bfloat16),
            pltpu.SemaphoreType.DMA((4,)),
        ],
        compiler_params=pltpu.CompilerParams(vmem_limit_bytes=VMEM),
        cost_estimate=pl.CostEstimate(flops=0, bytes_accessed=0, transcendentals=0),
    )(points, *blocks)


def picks_by_z(own, other, z):
    got = own + swap_core(other).astype(jnp.float32)
    got = got.reshape(SIDE, 2, -1, own.shape[1])

    def pick(d):
        return lax.dynamic_index_in_dim(got, (z + d) % SIDE, 0, keepdims=False)

    return [pick(0)] + [pick(d).astype(jnp.bfloat16) for d in (1, 3, 2)]


def sums_by_z(picked):
    pieces = picked[:1] + [send(v, hop_z(d)) for v, d in zip(picked[1:], (1, 3, 2))]
    return total(pieces).astype(jnp.bfloat16)


def owned(blocks, here, hop):
    def pick(d):
        return lax.dynamic_index_in_dim(blocks, (here + d) % SIDE, 1, keepdims=False)

    return [pick(0)] + [send(pick(d).astype(jnp.bfloat16), hop(d)) for d in (1, 3, 2)]


def total(pieces):
    out = pieces[0].astype(jnp.float32)
    for piece in pieces[1:]:
        out = out + piece.astype(jnp.float32)
    return out


def together(*pieces):
    return jnp.concatenate(pieces, axis=0)


def per_device(slopes, valid, sensor_map, reconstructor, fitting):
    s_idx = lax.axis_index("sens")
    l_idx = lax.axis_index("layer")
    z, c = s_idx // 2, s_idx % 2
    y, x = l_idx // SIDE, l_idx % SIDE
    width = slopes.shape[1]
    width_p = reconstructor.shape[0]
    act = fitting.shape[0]
    position = jnp.stack([c, y, x]).astype(jnp.int32)

    live = valid.astype(jnp.bfloat16)[None, :]
    masked = slopes * live
    late = lax.all_gather(
        jnp.pad(masked[PART:], ((0, 0), (0, WIDE - width))), "layer", axis=0, tiled=True
    )

    own_a = masked[:PART, :HALF]
    a_l, a_r = right(own_a), left(own_a)
    a_d, a_u = up(own_a), down(own_a)
    fits = [fitting, ring_z(fitting)]

    group = sensor_map * 2 + (lax.iota(jnp.int32, width) + s_idx * width) % 2
    lane = lax.iota(jnp.int32, 128)
    label = jnp.where(lane < LANES * (ROWS // PART), lane % 12, -1)
    member = ((group[None, :] == label[:, None]) & (valid[None, :] == 1)).astype(jnp.bfloat16)
    counted = jnp.concatenate([masked, jnp.ones((8, width), jnp.bfloat16)], axis=0)
    stats = nt(counted, member)
    stats = jnp.broadcast_to(stats[None], (8, *stats.shape))
    stats = jnp.sum(lax.all_to_all(stats, "sens", 0, 0, tiled=True), axis=0)
    means = stats[:ROWS] / jnp.maximum(stats[ROWS : ROWS + 1], 1.0)
    high = lax.reduce_precision(means, 8, 7)
    means = jnp.where((lane % LANES < 12)[None, :], high, means - high)
    means = sum(
        jnp.where((lane // LANES == q)[None, :], means[q * PART : (q + 1) * PART], 0.0)
        for q in range(ROWS // PART)
    ).astype(jnp.bfloat16)
    own_b = jnp.pad(masked[:PART, HALF:], ((0, 0), (0, 2 * HALF - width)))
    own_b = own_b + jnp.pad(means, ((0, 0), (MEANS, 0)))
    b_l, b_r = right(own_b), left(own_b)
    b_d, b_u = up(own_b), down(own_b)

    send_u = together(a_l, a_r, a_d)
    send_d = together(a_l, a_r, b_u)
    send_r = together(b_d, b_u, a_l)
    send_l = together(b_d, b_u, b_r)
    member, send_u, send_d, send_r, send_l, a_u, b_l = after(
        member, send_u, send_d, send_r, send_l, a_u, b_l
    )
    one_d, one_u = up(send_u), down(send_d)
    one_l, one_r = right(send_r), left(send_l)

    member, one_d, one_u, one_l, one_r = after(member, one_d, one_u, one_l, one_r)
    far_x_a, far_y_b = one_l[2 * PART :], one_u[2 * PART :]
    two_d = together(far_x_a, one_d[:PART])
    two_u = together(far_x_a, one_u[PART : 2 * PART])
    two_l = together(far_y_b, one_l[:PART])
    two_r = together(far_y_b, one_r[PART : 2 * PART])
    two_d, two_u, two_l, two_r = after(two_d, two_u, two_l, two_r)
    get_d, get_u = up(two_d), down(two_u)
    get_l, get_r = right(two_l), left(two_r)
    rw = -nt(reconstructor, member)
    rw_high = lax.reduce_precision(rw, 8, 7)
    rw_low = jnp.where((lane % LANES < 12)[None, :], rw - rw_high, 0.0)
    rw = jnp.concatenate([rw_high, rw_low], axis=1).astype(jnp.bfloat16)

    fits[1], rw, *ends = after(fits[1], rw, get_d[:PART], get_l[:PART])
    fits.append(ring_z(fits[-1]))
    end_d, end_l = up(ends[0]), right(ends[1])

    arrays = [own_a, own_b, a_l, b_l, a_r, b_r, a_d, b_d, a_u, b_u, one_d, one_u, one_l, one_r]
    arrays += [get_d, get_u, get_l, get_r, end_d, end_l]

    def piece(array, block, ry, rx, side):
        index = [i for i, a in enumerate(arrays) if a is array][0]
        return (index, block * PART, PART, ry, rx, side)

    pieces = []
    for ry, rx, (array_a, block_a), (array_b, block_b) in (
        (0, 0, (own_a, 0), (own_b, 0)),
        (0, 3, (a_l, 0), (b_l, 0)),
        (0, 1, (a_r, 0), (b_r, 0)),
        (3, 0, (a_d, 0), (b_d, 0)),
        (1, 0, (a_u, 0), (b_u, 0)),
        (3, 3, (one_d, 0), (one_l, 0)),
        (3, 1, (one_d, 1), (one_r, 0)),
        (1, 3, (one_u, 0), (one_l, 1)),
        (1, 1, (one_u, 1), (one_r, 1)),
        (0, 2, (one_l, 2), (one_r, 2)),
        (2, 0, (one_d, 2), (one_u, 2)),
        (3, 2, (get_d, 0), (get_l, 1)),
        (1, 2, (get_u, 0), (get_r, 1)),
        (2, 3, (get_d, 1), (get_l, 0)),
        (2, 1, (get_u, 1), (get_r, 0)),
        (2, 2, (end_d, 0), (end_l, 0)),
    ):
        pieces.append(piece(array_a, block_a, ry, rx, 0))
        pieces.append(piece(array_b, block_b, ry, rx, 1))
    own, other, tail = reconstruct(0, arrays, pieces, position, reconstructor, rw)
    own, other, *fits = after(own, other, *fits)
    fits.append(ring_z(fits[-1]))
    swapped = [swap_core(fits[0]), swap_core(fits[1])]
    near = sums_by_z(picks_by_z(own, other, z))
    near, fits[2], fits[3], *swapped = after(near, fits[2], fits[3], *swapped)
    swapped += [swap_core(fits[2]), swap_core(fits[3])]
    near, late, *swapped = after(near, late, *swapped)

    own, other = reconstruct(
        1, [late], [(0, 0, 16 * LATE, 0, 0, side) for side in (0, 1)],
        position, reconstructor, rw, tail,
    )
    far = sums_by_z(picks_by_z(own, other, z))
    points = jnp.concatenate([near, far], axis=1)

    rows = points.reshape(SIDE, SIDE, 8, width_p)
    rows = jnp.where(c == 0, rows, jnp.swapaxes(rows, 0, 1)).reshape(2 * ROWS, width_p)
    one = jnp.where(c == 0, y, x)
    two = jnp.where(c == 0, x, y)
    half_a = owned(fit(rows, fits).reshape(4, SIDE, SIDE * 8, act), one, hop_one)
    half_b = owned(fit(rows, swapped).reshape(4, SIDE, SIDE * 8, act), one, hop_one)
    both = jnp.concatenate([total(half_a), total(half_b)], axis=0)
    done = total(owned(both.reshape(8, SIDE, 8, act), two, hop_two))

    sens = lax.iota(jnp.int32, 8)
    step = jnp.where(sens % 2 == 0, z - sens // 2, sens // 2 - z) % SIDE
    found = jnp.where(sens % 2 == c, 0, 4) + step
    done = jnp.take(done, found, axis=0)
    return jnp.moveaxis(done, 0, 1).reshape(8, 8 * act)


def solution(mesh):
    placed = (P("layer", "sens"), P("sens"), P("sens"), P("layer", "sens"), P("sens", "layer"))
    return jax.shard_map(
        per_device,
        mesh=mesh,
        in_specs=placed,
        out_specs=P(("sens", "layer"), None),
        check_vma=False,
    )
```

```python
import functools

import jax
import jax.numpy as jnp
from jax import lax
from jax.experimental import pallas as pl
from jax.experimental.pallas import tpu as pltpu
from jax.sharding import PartitionSpec as P

SENSORS = 6
AXES = ("sens", "layer")
SIDE = 4
ROWS = 64
PART = 16
LATE = ROWS - PART
LANES = 24
HALF = 4096
EDGE = 3840
MEANS = 3968
WIDE = 8064
INSIDE = 14
PBLOCK = 256
VMEM = 52 * 2**20


def moved(fn):
    pairs = []
    for z in range(4):
        for c in range(2):
            for y in range(4):
                for x in range(4):
                    z2, c2, y2, x2 = fn(z, c, y, x)
                    pairs.append(
                        ((z * 2 + c) * 16 + y * 4 + x,
                         ((z2 % 4) * 2 + c2 % 2) * 16 + (y2 % 4) * 4 + x2 % 4)
                    )
    return pairs


def send(x, fn):
    return lax.ppermute(x, AXES, moved(fn))


def swap_core(v):
    return send(v, lambda z, c, y, x: (z, c + 1, y, x))


def right(v):
    return send(v, lambda z, c, y, x: (z, c, y, x + 1))


def left(v):
    return send(v, lambda z, c, y, x: (z, c, y, x - 1))


def up(v):
    return send(v, lambda z, c, y, x: (z, c, y + 1, x))


def down(v):
    return send(v, lambda z, c, y, x: (z, c, y - 1, x))


def hop_z(d):
    return lambda z, c, y, x: (z + d, c, y, x)


def hop_one(d):
    return lambda z, c, y, x: (z, c, y + d * (1 - c), x + d * c)


def hop_two(d):
    return lambda z, c, y, x: (z, c, y + d * c, x + d * (1 - c))


def ring_z(v):
    return send(v, lambda z, c, y, x: (z + 1 - 2 * c, c, y, x))


def after(value, *others):
    return lax.optimization_barrier((value, *others))


def nt(a, b, **kw):
    return lax.dot_general(
        a, b, (((1,), (1,)), ((), ())), preferred_element_type=jnp.float32, **kw
    )


def reconstruct_kernel(pieces, count, index, *refs):
    arrays = refs[:count]
    if index == 0:
        position, ra, rb, rw, own, other, tail, held, sems = refs[count:]
    else:
        position, ra, rb, rw, tail, own, other, held, sems = refs[count:]

    def copies(side):
        out = []
        for i, (a, row, rows, ry, rx, half) in enumerate(pieces):
            if half != side:
                continue
            if index == 0:
                y = lax.rem(position[1] + ry, SIDE)
                x = lax.rem(position[2] + rx, SIDE)
                to_row = pl.multiple_of((y * SIDE + x) * PART, PART)
                source = arrays[a].at[pl.ds(row, rows)]
                width = HALF
            else:
                to_row = row
                width = HALF if half == 0 else WIDE - HALF
                source = arrays[a].at[pl.ds(row, rows), pl.ds(half * HALF, width)]
            target = held.at[pl.ds(to_row, rows), pl.ds(half * HALF, width)]
            out.append(pltpu.make_async_copy(source, target, sems.at[i]))
        return out

    @pl.when(pl.program_id(0) == 0)
    def _():
        for copy in copies(0) + copies(1):
            copy.start()
        for copy in copies(0):
            copy.wait()

    val = nt(held[:, :HALF], ra[...])

    @pl.when(pl.program_id(0) == 0)
    def _():
        for copy in copies(1):
            copy.wait()

    lane = lax.broadcasted_iota(jnp.int32, (ra.shape[0], 128), 1)
    edge = rb[:, EDGE:MEANS].astype(jnp.float32)
    edge = jnp.where(lane < INSIDE, edge, 0.0).astype(jnp.bfloat16)
    val = val + nt(held[:, HALF : HALF + EDGE], rb[:, :EDGE])
    val = val + nt(held[:, HALF + EDGE : HALF + MEANS], edge)
    high, low = rw[:, :128].astype(jnp.float32), rw[:, 128:].astype(jnp.float32)

    def moved_by(means, q):
        chosen = (lane >= q * LANES) & (lane < (q + 1) * LANES)
        one = jnp.where(chosen, high, 0.0).astype(jnp.bfloat16)
        two = jnp.where(chosen, low, 0.0).astype(jnp.bfloat16)
        return nt(means, one) + nt(means, two)

    n, p = val.shape
    if index == 0:
        means = held[:, HALF + MEANS :]
        tail[...] = means
        val = val + moved_by(means, 0)
    else:
        means = tail[...]
        shift = [moved_by(means, q).reshape(16, 1, PART, p) for q in range(1, ROWS // PART)]
        val = val.reshape(16, LATE // PART, PART, p) + jnp.concatenate(shift, axis=1)
    pairs = val.reshape(SIDE, 2, n // 8, p)
    first = pairs[:, 0].reshape(n // 2, p)
    second = pairs[:, 1].reshape(n // 2, p)
    swapped = position[0] == 1
    own[...] = jnp.where(swapped, second, first)
    other[...] = jnp.where(swapped, first, second).astype(jnp.bfloat16)


def reconstruct(index, arrays, pieces, position, r, rw, tail=None):
    n = 16 * (PART if index == 0 else LATE)
    p = r.shape[0]
    half = pl.BlockSpec((n // 2, PBLOCK), lambda j: (0, j))
    whole = pl.BlockSpec((16 * PART, 128), lambda j: (0, 0))
    in_specs = [pl.BlockSpec(memory_space=pl.ANY)] * len(arrays) + [
        pl.BlockSpec(memory_space=pltpu.SMEM),
        pl.BlockSpec((PBLOCK, HALF), lambda j: (j, 0)),
        pl.BlockSpec((PBLOCK, HALF), lambda j: (j, 1)),
        pl.BlockSpec((PBLOCK, 256), lambda j: (j, 0)),
    ]
    args = [*arrays, position, r, r, rw]
    out_specs = [half, half]
    out_shape = [
        jax.ShapeDtypeStruct((n // 2, p), jnp.float32),
        jax.ShapeDtypeStruct((n // 2, p), jnp.bfloat16),
    ]
    if index == 0:
        out_specs.append(whole)
        out_shape.append(jax.ShapeDtypeStruct((16 * PART, 128), jnp.bfloat16))
    else:
        in_specs.append(whole)
        args.append(tail)
    return pl.pallas_call(
        functools.partial(reconstruct_kernel, tuple(pieces), len(arrays), index),
        grid=(pl.cdiv(p, PBLOCK),),
        in_specs=in_specs,
        out_specs=out_specs,
        out_shape=out_shape,
        scratch_shapes=[
            pltpu.VMEM((n, 2 * HALF), jnp.bfloat16),
            pltpu.SemaphoreType.DMA((len(pieces),)),
        ],
        compiler_params=pltpu.CompilerParams(vmem_limit_bytes=VMEM),
        cost_estimate=pl.CostEstimate(flops=0, bytes_accessed=0, transcendentals=0),
    )(*args)


def fit_kernel(p, f0, f1, f2, f3, out, held, sems):
    sources = (f0, f1, f2, f3)
    copies = [
        pltpu.make_async_copy(f, held.at[i], sems.at[i]) for i, f in enumerate(sources)
    ]
    for copy in copies:
        copy.start()
    for i, copy in enumerate(copies):
        copy.wait()
        out[i] = nt(p[...], held[i]).astype(jnp.bfloat16)


def fit(points, blocks):
    n, k = points.shape
    m = blocks[0].shape[0]
    return pl.pallas_call(
        fit_kernel,
        in_specs=[pl.BlockSpec(memory_space=pltpu.VMEM)]
        + [pl.BlockSpec(memory_space=pl.ANY)] * 4,
        out_specs=pl.BlockSpec(memory_space=pltpu.VMEM),
        out_shape=jax.ShapeDtypeStruct((4, n, m), jnp.bfloat16),
        scratch_shapes=[
            pltpu.VMEM((4, m, k), jnp.bfloat16),
            pltpu.SemaphoreType.DMA((4,)),
        ],
        compiler_params=pltpu.CompilerParams(vmem_limit_bytes=VMEM),
        cost_estimate=pl.CostEstimate(flops=0, bytes_accessed=0, transcendentals=0),
    )(points, *blocks)


def picks_by_z(own, other, z):
    got = own + swap_core(other).astype(jnp.float32)
    got = got.reshape(SIDE, 2, -1, own.shape[1])

    def pick(d):
        return lax.dynamic_index_in_dim(got, (z + d) % SIDE, 0, keepdims=False)

    return [pick(0)] + [pick(d).astype(jnp.bfloat16) for d in (1, 3, 2)]


def sums_by_z(picked):
    pieces = picked[:1] + [send(v, hop_z(d)) for v, d in zip(picked[1:], (1, 3, 2))]
    return total(pieces).astype(jnp.bfloat16)


def owned(blocks, here, hop):
    def pick(d):
        return lax.dynamic_index_in_dim(blocks, (here + d) % SIDE, 1, keepdims=False)

    return [pick(0)] + [send(pick(d).astype(jnp.bfloat16), hop(d)) for d in (1, 3, 2)]


def total(pieces):
    out = pieces[0].astype(jnp.float32)
    for piece in pieces[1:]:
        out = out + piece.astype(jnp.float32)
    return out


def together(*pieces):
    return jnp.concatenate(pieces, axis=0)


def per_device(slopes, valid, sensor_map, reconstructor, fitting):
    s_idx = lax.axis_index("sens")
    l_idx = lax.axis_index("layer")
    z, c = s_idx // 2, s_idx % 2
    y, x = l_idx // SIDE, l_idx % SIDE
    width = slopes.shape[1]
    width_p = reconstructor.shape[0]
    act = fitting.shape[0]
    position = jnp.stack([c, y, x]).astype(jnp.int32)

    live = valid.astype(jnp.bfloat16)[None, :]
    masked = slopes * live
    late = lax.all_gather(
        jnp.pad(masked[PART:], ((0, 0), (0, WIDE - width))), "layer", axis=0, tiled=True
    )

    own_a = masked[:PART, :HALF]
    a_l, a_r = right(own_a), left(own_a)
    a_d, a_u = up(own_a), down(own_a)
    fits = [fitting, ring_z(fitting)]

    group = sensor_map * 2 + (lax.iota(jnp.int32, width) + s_idx * width) % 2
    lane = lax.iota(jnp.int32, 128)
    label = jnp.where(lane < LANES * (ROWS // PART), lane % 12, -1)
    member = ((group[None, :] == label[:, None]) & (valid[None, :] == 1)).astype(jnp.bfloat16)
    counted = jnp.concatenate([masked, jnp.ones((8, width), jnp.bfloat16)], axis=0)
    stats = nt(counted, member)
    stats = jnp.broadcast_to(stats[None], (8, *stats.shape))
    stats = jnp.sum(lax.all_to_all(stats, "sens", 0, 0, tiled=True), axis=0)
    means = stats[:ROWS] / jnp.maximum(stats[ROWS : ROWS + 1], 1.0)
    high = lax.reduce_precision(means, 8, 7)
    means = jnp.where((lane % LANES < 12)[None, :], high, means - high)
    means = sum(
        jnp.where((lane // LANES == q)[None, :], means[q * PART : (q + 1) * PART], 0.0)
        for q in range(ROWS // PART)
    ).astype(jnp.bfloat16)
    own_b = jnp.pad(masked[:PART, HALF:], ((0, 0), (0, 2 * HALF - width)))
    own_b = own_b + jnp.pad(means, ((0, 0), (MEANS, 0)))
    b_l, b_r = right(own_b), left(own_b)
    b_d, b_u = up(own_b), down(own_b)

    send_u = together(a_l, a_r, a_d)
    send_d = together(a_l, a_r, b_u)
    send_r = together(b_d, b_u, a_l)
    send_l = together(b_d, b_u, b_r)
    fits[1], send_u, send_d, send_r, send_l, a_u, b_l = after(
        fits[1], send_u, send_d, send_r, send_l, a_u, b_l
    )
    fits.append(ring_z(fits[-1]))
    one_d, one_u = up(send_u), down(send_d)
    one_l, one_r = right(send_r), left(send_l)

    member, fits[2], one_d, one_u, one_l, one_r = after(
        member, fits[2], one_d, one_u, one_l, one_r
    )
    fits.append(ring_z(fits[-1]))
    far_x_a, far_y_b = one_l[2 * PART :], one_u[2 * PART :]
    two_d = together(far_x_a, one_d[:PART])
    two_u = together(far_x_a, one_u[PART : 2 * PART])
    two_l = together(far_y_b, one_l[:PART])
    two_r = together(far_y_b, one_r[PART : 2 * PART])
    two_d, two_u, two_l, two_r = after(two_d, two_u, two_l, two_r)
    get_d, get_u = up(two_d), down(two_u)
    get_l, get_r = right(two_l), left(two_r)
    rw = -nt(reconstructor, member)
    rw_high = lax.reduce_precision(rw, 8, 7)
    rw_low = jnp.where((lane % LANES < 12)[None, :], rw - rw_high, 0.0)
    rw = jnp.concatenate([rw_high, rw_low], axis=1).astype(jnp.bfloat16)

    rw, get_u, get_r, *ends = after(rw, get_u, get_r, get_d[:PART], get_l[:PART])
    end_d, end_l = up(ends[0]), right(ends[1])
    end_d, end_l, *fits = after(end_d, end_l, *fits)

    arrays = [own_a, own_b, a_l, b_l, a_r, b_r, a_d, b_d, a_u, b_u, one_d, one_u, one_l, one_r]
    arrays += [get_d, get_u, get_l, get_r, end_d, end_l]

    def piece(array, block, ry, rx, side):
        index = [i for i, a in enumerate(arrays) if a is array][0]
        return (index, block * PART, PART, ry, rx, side)

    pieces = []
    for ry, rx, (array_a, block_a), (array_b, block_b) in (
        (0, 0, (own_a, 0), (own_b, 0)),
        (0, 3, (a_l, 0), (b_l, 0)),
        (0, 1, (a_r, 0), (b_r, 0)),
        (3, 0, (a_d, 0), (b_d, 0)),
        (1, 0, (a_u, 0), (b_u, 0)),
        (3, 3, (one_d, 0), (one_l, 0)),
        (3, 1, (one_d, 1), (one_r, 0)),
        (1, 3, (one_u, 0), (one_l, 1)),
        (1, 1, (one_u, 1), (one_r, 1)),
        (0, 2, (one_l, 2), (one_r, 2)),
        (2, 0, (one_d, 2), (one_u, 2)),
        (3, 2, (get_d, 0), (get_l, 1)),
        (1, 2, (get_u, 0), (get_r, 1)),
        (2, 3, (get_d, 1), (get_l, 0)),
        (2, 1, (get_u, 1), (get_r, 0)),
        (2, 2, (end_d, 0), (end_l, 0)),
    ):
        pieces.append(piece(array_a, block_a, ry, rx, 0))
        pieces.append(piece(array_b, block_b, ry, rx, 1))
    own, other, tail = reconstruct(0, arrays, pieces, position, reconstructor, rw)
    swapped = [swap_core(f) for f in fits]
    own, other, *swapped = after(own, other, *swapped)
    near = sums_by_z(picks_by_z(own, other, z))
    near, late = after(near, late)

    own, other = reconstruct(
        1, [late], [(0, 0, 16 * LATE, 0, 0, side) for side in (0, 1)],
        position, reconstructor, rw, tail,
    )
    far = sums_by_z(picks_by_z(own, other, z))
    points = jnp.concatenate([near, far], axis=1)

    rows = points.reshape(SIDE, SIDE, 8, width_p)
    rows = jnp.where(c == 0, rows, jnp.swapaxes(rows, 0, 1)).reshape(2 * ROWS, width_p)
    one = jnp.where(c == 0, y, x)
    two = jnp.where(c == 0, x, y)
    half_a = owned(fit(rows, fits).reshape(4, SIDE, SIDE * 8, act), one, hop_one)
    half_b = owned(fit(rows, swapped).reshape(4, SIDE, SIDE * 8, act), one, hop_one)
    both = jnp.concatenate([total(half_a), total(half_b)], axis=0)
    done = total(owned(both.reshape(8, SIDE, 8, act), two, hop_two))

    sens = lax.iota(jnp.int32, 8)
    step = jnp.where(sens % 2 == 0, z - sens // 2, sens // 2 - z) % SIDE
    found = jnp.where(sens % 2 == c, 0, 4) + step
    done = jnp.take(done, found, axis=0)
    return jnp.moveaxis(done, 0, 1).reshape(8, 8 * act)


def solution(mesh):
    placed = (P("layer", "sens"), P("sens"), P("sens"), P("layer", "sens"), P("sens", "layer"))
    return jax.shard_map(
        per_device,
        mesh=mesh,
        in_specs=placed,
        out_specs=P(("sens", "layer"), None),
        check_vma=False,
    )
```

```python
import functools

import jax
import jax.numpy as jnp
from jax import lax
from jax.experimental import pallas as pl
from jax.experimental.pallas import tpu as pltpu
from jax.sharding import PartitionSpec as P

SENSORS = 6
AXES = ("sens", "layer")
SIDE = 4
ROWS = 64
VMEM = 52 * 2**20


def moved(fn):
    pairs = []
    for z in range(4):
        for c in range(2):
            for y in range(4):
                for x in range(4):
                    z2, c2, y2, x2 = fn(z, c, y, x)
                    pairs.append(
                        ((z * 2 + c) * 16 + y * 4 + x,
                         ((z2 % 4) * 2 + c2 % 2) * 16 + (y2 % 4) * 4 + x2 % 4)
                    )
    return pairs


def send(x, fn):
    return lax.ppermute(x, AXES, moved(fn))


def swap_core(v):
    return send(v, lambda z, c, y, x: (z, c + 1, y, x))


def ring_z(v):
    return send(v, lambda z, c, y, x: (z + 1 - 2 * c, c, y, x))


def hop_x(d):
    return lambda z, c, y, x: (z, c, y, x + d)


def hop_y(d):
    return lambda z, c, y, x: (z, c, y + d, x)


def hop_z(d):
    return lambda z, c, y, x: (z + d, c, y, x)


def hop_one(d):
    return lambda z, c, y, x: (z, c, y + d * (1 - c), x + d * c)


def hop_two(d):
    return lambda z, c, y, x: (z, c, y + d * c, x + d * (1 - c))


def after(value, *others):
    return lax.optimization_barrier((value, *others))


def nt(a, b, **kw):
    return lax.dot_general(
        a, b, (((1,), (1,)), ((), ())), preferred_element_type=jnp.float32, **kw
    )


def fit_kernel(p, *refs):
    count = len(refs) - 3
    sources, (out, held, sems) = refs[:count], refs[count:]
    copies = [
        pltpu.make_async_copy(f, held.at[i], sems.at[i]) for i, f in enumerate(sources)
    ]
    for copy in copies:
        copy.start()
    for i, copy in enumerate(copies):
        copy.wait()
        out[i] = nt(p[...], held[i]).astype(jnp.bfloat16)


def fit(points, blocks):
    n, k = points.shape
    m = blocks[0].shape[0]
    count = len(blocks)
    return pl.pallas_call(
        fit_kernel,
        in_specs=[pl.BlockSpec(memory_space=pltpu.VMEM)]
        + [pl.BlockSpec(memory_space=pl.ANY)] * count,
        out_specs=pl.BlockSpec(memory_space=pltpu.VMEM),
        out_shape=jax.ShapeDtypeStruct((count, n, m), jnp.bfloat16),
        scratch_shapes=[
            pltpu.VMEM((count, m, k), jnp.bfloat16),
            pltpu.SemaphoreType.DMA((count,)),
        ],
        compiler_params=pltpu.CompilerParams(vmem_limit_bytes=VMEM),
        cost_estimate=pl.CostEstimate(flops=0, bytes_accessed=0, transcendentals=0),
    )(points, *blocks)


def sums_by_sens(full, z, c):
    halves = full.reshape(SIDE, 2, 2 * ROWS, full.shape[1])

    def core(i):
        return lax.dynamic_index_in_dim(halves, i, 1, keepdims=False)

    got = core(c) + swap_core(core(1 - c).astype(jnp.bfloat16)).astype(jnp.float32)

    def pick(d):
        return lax.dynamic_index_in_dim(got, (z + d) % SIDE, 0, keepdims=False)

    pieces = [pick(0)] + [send(pick(d).astype(jnp.bfloat16), hop_z(d)) for d in (1, 3, 2)]
    return total(pieces).astype(jnp.bfloat16)


def owned(blocks, here, hop):
    def pick(d):
        return lax.dynamic_index_in_dim(blocks, (here + d) % SIDE, 1, keepdims=False)

    return [pick(0)] + [send(pick(d).astype(jnp.bfloat16), hop(d)) for d in (1, 3, 2)]


def total(pieces):
    out = pieces[0].astype(jnp.float32)
    for piece in pieces[1:]:
        out = out + piece.astype(jnp.float32)
    return out


def per_device(slopes, valid, sensor_map, reconstructor, fitting):
    s_idx = lax.axis_index("sens")
    l_idx = lax.axis_index("layer")
    z, c = s_idx // 2, s_idx % 2
    y, x = l_idx // SIDE, l_idx % SIDE
    width = slopes.shape[1]
    width_p = reconstructor.shape[0]
    act = fitting.shape[0]

    masked = slopes * valid.astype(jnp.bfloat16)[None, :]
    whole = lax.all_gather(masked, "layer", axis=0, tiled=True)
    fits = [fitting, ring_z(fitting)]

    group = sensor_map * 2 + (lax.iota(jnp.int32, width) + s_idx * width) % 2
    lane = lax.iota(jnp.int32, 128)
    label = jnp.where(lane < 36, lane % 12, -1)
    member = ((group[None, :] == label[:, None]) & (valid[None, :] == 1)).astype(jnp.bfloat16)
    counted = jnp.concatenate([masked, jnp.ones((8, width), jnp.bfloat16)], axis=0)
    stats = nt(counted, member)
    stats = jnp.broadcast_to(stats[None], (8, *stats.shape))
    stats = jnp.sum(lax.all_to_all(stats, "sens", 0, 0, tiled=True), axis=0)
    means = stats[:ROWS] / jnp.maximum(stats[ROWS : ROWS + 1], 1.0)
    high = lax.reduce_precision(means, 8, 7)
    low = (lane >= 12) & (lane < 24)
    means = jnp.where(low[None, :], means - high, high).astype(jnp.bfloat16)

    along = jnp.stack([means] + [send(means, hop_x(d)) for d in (1, 2, 3)])
    along = jnp.take(along, (x - jnp.arange(SIDE)) % SIDE, axis=0, mode="clip")
    means = jnp.stack([along] + [send(along, hop_y(d)) for d in (1, 2, 3)])
    means = jnp.take(means, (y - jnp.arange(SIDE)) % SIDE, axis=0, mode="clip")
    means = means.reshape(16 * ROWS, 128)
    fits[1], member, means = after(fits[1], member, means)
    fits.append(ring_z(fits[-1]))

    rw = -nt(reconstructor, member)
    rw_high = lax.reduce_precision(rw, 8, 7)
    last = (lane >= 24) & (lane < 36)
    rw = jnp.where(last[None, :], rw - rw_high, rw_high).astype(jnp.bfloat16)
    fits[2], rw = after(fits[2], rw)
    fits.append(ring_z(fits[-1]))
    shift = nt(means, rw)
    shift, *fits = after(shift, *fits)
    swapped = [swap_core(f) for f in fits]
    shift, whole, *swapped = after(shift, whole, *swapped)

    points = sums_by_sens(nt(whole, reconstructor) + shift, z, c)

    rows = points.reshape(SIDE, SIDE, 8, width_p)
    rows = jnp.where(c == 0, rows, jnp.swapaxes(rows, 0, 1)).reshape(2 * ROWS, width_p)
    one = jnp.where(c == 0, y, x)
    two = jnp.where(c == 0, x, y)
    first = fit(rows, fits + swapped[:1])
    first, rows = after(first, rows)
    half_a = owned(first.reshape(5, SIDE, SIDE * 8, act), one, hop_one)
    half_b = owned(fit(rows, swapped[1:]).reshape(3, SIDE, SIDE * 8, act), one, hop_one)
    both = jnp.concatenate([total(half_a), total(half_b)], axis=0)
    done = total(owned(both.reshape(8, SIDE, 8, act), two, hop_two))

    sens = lax.iota(jnp.int32, 8)
    step = jnp.where(sens % 2 == 0, z - sens // 2, sens // 2 - z) % SIDE
    found = jnp.where(sens % 2 == c, 0, 4) + step
    done = jnp.take(done, found, axis=0, mode="clip")
    return jnp.moveaxis(done, 0, 1).reshape(8, 8 * act)


def solution(mesh):
    placed = (P("layer", "sens"), P("sens"), P("sens"), P("layer", "sens"), P("sens", "layer"))
    return jax.shard_map(
        per_device,
        mesh=mesh,
        in_specs=placed,
        out_specs=P(("sens", "layer"), None),
        check_vma=False,
    )
```

```python
import functools

import jax
import jax.numpy as jnp
from jax import lax
from jax.experimental import pallas as pl
from jax.experimental.pallas import tpu as pltpu
from jax.sharding import PartitionSpec as P

SENSORS = 6
AXES = ("sens", "layer")
SIDE = 4
ROWS = 64
PART = 16
LATE = ROWS - PART
LANES = 24
HALF = 4096
EDGE = 3840
MEANS = 3968
WIDE = 8064
INSIDE = 14
PBLOCK = 256
VMEM = 52 * 2**20


def moved(fn):
    pairs = []
    for z in range(4):
        for c in range(2):
            for y in range(4):
                for x in range(4):
                    z2, c2, y2, x2 = fn(z, c, y, x)
                    pairs.append(
                        ((z * 2 + c) * 16 + y * 4 + x,
                         ((z2 % 4) * 2 + c2 % 2) * 16 + (y2 % 4) * 4 + x2 % 4)
                    )
    return pairs


def send(x, fn):
    return lax.ppermute(x, AXES, moved(fn))


def swap_core(v):
    return send(v, lambda z, c, y, x: (z, c + 1, y, x))


def right(v):
    return send(v, lambda z, c, y, x: (z, c, y, x + 1))


def left(v):
    return send(v, lambda z, c, y, x: (z, c, y, x - 1))


def up(v):
    return send(v, lambda z, c, y, x: (z, c, y + 1, x))


def down(v):
    return send(v, lambda z, c, y, x: (z, c, y - 1, x))


def hop_z(d):
    return lambda z, c, y, x: (z + d, c, y, x)


def hop_one(d):
    return lambda z, c, y, x: (z, c, y + d * (1 - c), x + d * c)


def hop_two(d):
    return lambda z, c, y, x: (z, c, y + d * c, x + d * (1 - c))


def ring_z(v):
    return send(v, lambda z, c, y, x: (z + 1 - 2 * c, c, y, x))


def after(value, *others):
    return lax.optimization_barrier((value, *others))


def nt(a, b, **kw):
    return lax.dot_general(
        a, b, (((1,), (1,)), ((), ())), preferred_element_type=jnp.float32, **kw
    )


def reconstruct_kernel(pieces, count, index, *refs):
    arrays = refs[:count]
    if index == 0:
        position, ra, rb, rw, own, other, tail, held, sems = refs[count:]
    else:
        position, ra, rb, rw, tail, own, other, held, sems = refs[count:]

    def copies(side):
        out = []
        for i, (a, row, rows, ry, rx, half) in enumerate(pieces):
            if half != side:
                continue
            if index == 0:
                y = lax.rem(position[1] + ry, SIDE)
                x = lax.rem(position[2] + rx, SIDE)
                to_row = pl.multiple_of((y * SIDE + x) * PART, PART)
                source = arrays[a].at[pl.ds(row, rows)]
                width = HALF
            else:
                to_row = row
                width = HALF if half == 0 else WIDE - HALF
                source = arrays[a].at[pl.ds(row, rows), pl.ds(half * HALF, width)]
            target = held.at[pl.ds(to_row, rows), pl.ds(half * HALF, width)]
            out.append(pltpu.make_async_copy(source, target, sems.at[i]))
        return out

    @pl.when(pl.program_id(0) == 0)
    def _():
        for copy in copies(0) + copies(1):
            copy.start()
        for copy in copies(0):
            copy.wait()

    val = nt(held[:, :HALF], ra[...])

    @pl.when(pl.program_id(0) == 0)
    def _():
        for copy in copies(1):
            copy.wait()

    lane = lax.broadcasted_iota(jnp.int32, (ra.shape[0], 128), 1)
    edge = rb[:, EDGE:MEANS].astype(jnp.float32)
    edge = jnp.where(lane < INSIDE, edge, 0.0).astype(jnp.bfloat16)
    val = val + nt(held[:, HALF : HALF + EDGE], rb[:, :EDGE])
    val = val + nt(held[:, HALF + EDGE : HALF + MEANS], edge)
    high, low = rw[:, :128].astype(jnp.float32), rw[:, 128:].astype(jnp.float32)

    def moved_by(means, q):
        chosen = (lane >= q * LANES) & (lane < (q + 1) * LANES)
        one = jnp.where(chosen, high, 0.0).astype(jnp.bfloat16)
        two = jnp.where(chosen, low, 0.0).astype(jnp.bfloat16)
        return nt(means, one) + nt(means, two)

    n, p = val.shape
    if index == 0:
        means = held[:, HALF + MEANS :]
        tail[...] = means
        val = val + moved_by(means, 0)
    else:
        means = tail[...]
        shift = [moved_by(means, q).reshape(16, 1, PART, p) for q in range(1, ROWS // PART)]
        val = val.reshape(16, LATE // PART, PART, p) + jnp.concatenate(shift, axis=1)
    pairs = val.reshape(SIDE, 2, n // 8, p)
    first = pairs[:, 0].reshape(n // 2, p)
    second = pairs[:, 1].reshape(n // 2, p)
    swapped = position[0] == 1
    own[...] = jnp.where(swapped, second, first)
    other[...] = jnp.where(swapped, first, second).astype(jnp.bfloat16)


def reconstruct(index, arrays, pieces, position, r, rw, tail=None):
    n = 16 * (PART if index == 0 else LATE)
    p = r.shape[0]
    half = pl.BlockSpec((n // 2, PBLOCK), lambda j: (0, j))
    whole = pl.BlockSpec((16 * PART, 128), lambda j: (0, 0))
    in_specs = [pl.BlockSpec(memory_space=pl.ANY)] * len(arrays) + [
        pl.BlockSpec(memory_space=pltpu.SMEM),
        pl.BlockSpec((PBLOCK, HALF), lambda j: (j, 0)),
        pl.BlockSpec((PBLOCK, HALF), lambda j: (j, 1)),
        pl.BlockSpec((PBLOCK, 256), lambda j: (j, 0)),
    ]
    args = [*arrays, position, r, r, rw]
    out_specs = [half, half]
    out_shape = [
        jax.ShapeDtypeStruct((n // 2, p), jnp.float32),
        jax.ShapeDtypeStruct((n // 2, p), jnp.bfloat16),
    ]
    if index == 0:
        out_specs.append(whole)
        out_shape.append(jax.ShapeDtypeStruct((16 * PART, 128), jnp.bfloat16))
    else:
        in_specs.append(whole)
        args.append(tail)
    return pl.pallas_call(
        functools.partial(reconstruct_kernel, tuple(pieces), len(arrays), index),
        grid=(pl.cdiv(p, PBLOCK),),
        in_specs=in_specs,
        out_specs=out_specs,
        out_shape=out_shape,
        scratch_shapes=[
            pltpu.VMEM((n, 2 * HALF), jnp.bfloat16),
            pltpu.SemaphoreType.DMA((len(pieces),)),
        ],
        compiler_params=pltpu.CompilerParams(vmem_limit_bytes=VMEM),
        cost_estimate=pl.CostEstimate(flops=0, bytes_accessed=0, transcendentals=0),
    )(*args)


def fit_kernel(p, *refs):
    count = len(refs) - 3
    sources, (out, held, sems) = refs[:count], refs[count:]
    copies = [
        pltpu.make_async_copy(f, held.at[i], sems.at[i]) for i, f in enumerate(sources)
    ]
    for copy in copies:
        copy.start()
    for i, copy in enumerate(copies):
        copy.wait()
        out[i] = nt(p[...], held[i]).astype(jnp.bfloat16)


def fit(points, blocks):
    n, k = points.shape
    m = blocks[0].shape[0]
    count = len(blocks)
    return pl.pallas_call(
        fit_kernel,
        in_specs=[pl.BlockSpec(memory_space=pltpu.VMEM)]
        + [pl.BlockSpec(memory_space=pl.ANY)] * count,
        out_specs=pl.BlockSpec(memory_space=pltpu.VMEM),
        out_shape=jax.ShapeDtypeStruct((count, n, m), jnp.bfloat16),
        scratch_shapes=[
            pltpu.VMEM((count, m, k), jnp.bfloat16),
            pltpu.SemaphoreType.DMA((count,)),
        ],
        compiler_params=pltpu.CompilerParams(vmem_limit_bytes=VMEM),
        cost_estimate=pl.CostEstimate(flops=0, bytes_accessed=0, transcendentals=0),
    )(points, *blocks)


def picks_by_z(own, other, z):
    got = own + swap_core(other).astype(jnp.float32)
    got = got.reshape(SIDE, 2, -1, own.shape[1])

    def pick(d):
        return lax.dynamic_index_in_dim(got, (z + d) % SIDE, 0, keepdims=False)

    return [pick(0)] + [pick(d).astype(jnp.bfloat16) for d in (1, 3, 2)]


def sums_by_z(picked):
    pieces = picked[:1] + [send(v, hop_z(d)) for v, d in zip(picked[1:], (1, 3, 2))]
    return total(pieces).astype(jnp.bfloat16)


def owned(blocks, here, hop):
    def pick(d):
        return lax.dynamic_index_in_dim(blocks, (here + d) % SIDE, 1, keepdims=False)

    return [pick(0)] + [send(pick(d).astype(jnp.bfloat16), hop(d)) for d in (1, 3, 2)]


def total(pieces):
    out = pieces[0].astype(jnp.float32)
    for piece in pieces[1:]:
        out = out + piece.astype(jnp.float32)
    return out


def together(*pieces):
    return jnp.concatenate(pieces, axis=0)


def per_device(slopes, valid, sensor_map, reconstructor, fitting):
    s_idx = lax.axis_index("sens")
    l_idx = lax.axis_index("layer")
    z, c = s_idx // 2, s_idx % 2
    y, x = l_idx // SIDE, l_idx % SIDE
    width = slopes.shape[1]
    width_p = reconstructor.shape[0]
    act = fitting.shape[0]
    position = jnp.stack([c, y, x]).astype(jnp.int32)

    live = valid.astype(jnp.bfloat16)[None, :]
    masked = slopes * live
    late = lax.all_gather(
        jnp.pad(masked[PART:], ((0, 0), (0, WIDE - width))), "layer", axis=0, tiled=True
    )

    own_a = masked[:PART, :HALF]
    a_l, a_r = right(own_a), left(own_a)
    a_d, a_u = up(own_a), down(own_a)
    fits = [fitting, ring_z(fitting)]

    group = sensor_map * 2 + (lax.iota(jnp.int32, width) + s_idx * width) % 2
    lane = lax.iota(jnp.int32, 128)
    label = jnp.where(lane < LANES * (ROWS // PART), lane % 12, -1)
    member = ((group[None, :] == label[:, None]) & (valid[None, :] == 1)).astype(jnp.bfloat16)
    counted = jnp.concatenate([masked, jnp.ones((8, width), jnp.bfloat16)], axis=0)
    stats = nt(counted, member)
    stats = jnp.broadcast_to(stats[None], (8, *stats.shape))
    stats = jnp.sum(lax.all_to_all(stats, "sens", 0, 0, tiled=True), axis=0)
    means = stats[:ROWS] / jnp.maximum(stats[ROWS : ROWS + 1], 1.0)
    high = lax.reduce_precision(means, 8, 7)
    means = jnp.where((lane % LANES < 12)[None, :], high, means - high)
    means = sum(
        jnp.where((lane // LANES == q)[None, :], means[q * PART : (q + 1) * PART], 0.0)
        for q in range(ROWS // PART)
    ).astype(jnp.bfloat16)
    own_b = jnp.pad(masked[:PART, HALF:], ((0, 0), (0, 2 * HALF - width)))
    own_b = own_b + jnp.pad(means, ((0, 0), (MEANS, 0)))
    b_l, b_r = right(own_b), left(own_b)
    b_d, b_u = up(own_b), down(own_b)

    send_u = together(a_l, a_r, a_d)
    send_d = together(a_l, a_r, b_u)
    send_r = together(b_d, b_u, a_l)
    send_l = together(b_d, b_u, b_r)
    fits[1], send_u, send_d, send_r, send_l, a_u, b_l = after(
        fits[1], send_u, send_d, send_r, send_l, a_u, b_l
    )
    fits.append(ring_z(fits[-1]))
    one_d, one_u = up(send_u), down(send_d)
    one_l, one_r = right(send_r), left(send_l)

    member, fits[2], one_d, one_u, one_l, one_r = after(
        member, fits[2], one_d, one_u, one_l, one_r
    )
    fits.append(ring_z(fits[-1]))
    far_x_a, far_y_b = one_l[2 * PART :], one_u[2 * PART :]
    two_d = together(far_x_a, one_d[:PART])
    two_u = together(far_x_a, one_u[PART : 2 * PART])
    two_l = together(far_y_b, one_l[:PART])
    two_r = together(far_y_b, one_r[PART : 2 * PART])
    two_d, two_u, two_l, two_r = after(two_d, two_u, two_l, two_r)
    get_d, get_u = up(two_d), down(two_u)
    get_l, get_r = right(two_l), left(two_r)
    rw = -nt(reconstructor, member)
    rw_high = lax.reduce_precision(rw, 8, 7)
    rw_low = jnp.where((lane % LANES < 12)[None, :], rw - rw_high, 0.0)
    rw = jnp.concatenate([rw_high, rw_low], axis=1).astype(jnp.bfloat16)

    rw, get_u, get_r, *ends = after(rw, get_u, get_r, get_d[:PART], get_l[:PART])
    end_d, end_l = up(ends[0]), right(ends[1])
    end_d, end_l, *fits = after(end_d, end_l, *fits)

    arrays = [own_a, own_b, a_l, b_l, a_r, b_r, a_d, b_d, a_u, b_u, one_d, one_u, one_l, one_r]
    arrays += [get_d, get_u, get_l, get_r, end_d, end_l]

    def piece(array, block, ry, rx, side):
        index = [i for i, a in enumerate(arrays) if a is array][0]
        return (index, block * PART, PART, ry, rx, side)

    pieces = []
    for ry, rx, (array_a, block_a), (array_b, block_b) in (
        (0, 0, (own_a, 0), (own_b, 0)),
        (0, 3, (a_l, 0), (b_l, 0)),
        (0, 1, (a_r, 0), (b_r, 0)),
        (3, 0, (a_d, 0), (b_d, 0)),
        (1, 0, (a_u, 0), (b_u, 0)),
        (3, 3, (one_d, 0), (one_l, 0)),
        (3, 1, (one_d, 1), (one_r, 0)),
        (1, 3, (one_u, 0), (one_l, 1)),
        (1, 1, (one_u, 1), (one_r, 1)),
        (0, 2, (one_l, 2), (one_r, 2)),
        (2, 0, (one_d, 2), (one_u, 2)),
        (3, 2, (get_d, 0), (get_l, 1)),
        (1, 2, (get_u, 0), (get_r, 1)),
        (2, 3, (get_d, 1), (get_l, 0)),
        (2, 1, (get_u, 1), (get_r, 0)),
        (2, 2, (end_d, 0), (end_l, 0)),
    ):
        pieces.append(piece(array_a, block_a, ry, rx, 0))
        pieces.append(piece(array_b, block_b, ry, rx, 1))
    own, other, tail = reconstruct(0, arrays, pieces, position, reconstructor, rw)
    swapped = [swap_core(f) for f in fits]
    own, other, *swapped = after(own, other, *swapped)
    picked = picks_by_z(own, other, z)
    *picked, late = after(*picked, late)
    near = sums_by_z(picked)

    own, other = reconstruct(
        1, [late], [(0, 0, 16 * LATE, 0, 0, side) for side in (0, 1)],
        position, reconstructor, rw, tail,
    )
    own, other, near = after(own, other, near)
    far = sums_by_z(picks_by_z(own, other, z))
    points = jnp.concatenate([near, far], axis=1)

    rows = points.reshape(SIDE, SIDE, 8, width_p)
    rows = jnp.where(c == 0, rows, jnp.swapaxes(rows, 0, 1)).reshape(2 * ROWS, width_p)
    one = jnp.where(c == 0, y, x)
    two = jnp.where(c == 0, x, y)
    half_a = owned(fit(rows, fits).reshape(4, SIDE, SIDE * 8, act), one, hop_one)
    half_b = owned(fit(rows, swapped).reshape(4, SIDE, SIDE * 8, act), one, hop_one)
    both = jnp.concatenate([total(half_a), total(half_b)], axis=0)
    done = total(owned(both.reshape(8, SIDE, 8, act), two, hop_two))

    sens = lax.iota(jnp.int32, 8)
    step = jnp.where(sens % 2 == 0, z - sens // 2, sens // 2 - z) % SIDE
    found = jnp.where(sens % 2 == c, 0, 4) + step
    done = jnp.take(done, found, axis=0, mode="clip")
    return jnp.moveaxis(done, 0, 1).reshape(8, 8 * act)


def solution(mesh):
    placed = (P("layer", "sens"), P("sens"), P("sens"), P("layer", "sens"), P("sens", "layer"))
    return jax.shard_map(
        per_device,
        mesh=mesh,
        in_specs=placed,
        out_specs=P(("sens", "layer"), None),
        check_vma=False,
    )
```

```python
import functools

import jax
import jax.numpy as jnp
from jax import lax
from jax.experimental import pallas as pl
from jax.experimental.pallas import tpu as pltpu
from jax.sharding import PartitionSpec as P

SENSORS = 6
AXES = ("sens", "layer")
SIDE = 4
ROWS = 64
PART = 16
LATE = ROWS - PART
LANES = 24
HALF = 4096
EDGE = 3840
MEANS = 3968
WIDE = 8064
INSIDE = 14
PBLOCK = 256
VMEM = 52 * 2**20


def moved(fn):
    pairs = []
    for z in range(4):
        for c in range(2):
            for y in range(4):
                for x in range(4):
                    z2, c2, y2, x2 = fn(z, c, y, x)
                    pairs.append(
                        ((z * 2 + c) * 16 + y * 4 + x,
                         ((z2 % 4) * 2 + c2 % 2) * 16 + (y2 % 4) * 4 + x2 % 4)
                    )
    return pairs


def send(x, fn):
    return lax.ppermute(x, AXES, moved(fn))


def swap_core(v):
    return send(v, lambda z, c, y, x: (z, c + 1, y, x))


def right(v):
    return send(v, lambda z, c, y, x: (z, c, y, x + 1))


def left(v):
    return send(v, lambda z, c, y, x: (z, c, y, x - 1))


def up(v):
    return send(v, lambda z, c, y, x: (z, c, y + 1, x))


def down(v):
    return send(v, lambda z, c, y, x: (z, c, y - 1, x))


def hop_z(d):
    return lambda z, c, y, x: (z + d, c, y, x)


def hop_one(d):
    return lambda z, c, y, x: (z, c, y + d * (1 - c), x + d * c)


def hop_two(d):
    return lambda z, c, y, x: (z, c, y + d * c, x + d * (1 - c))


def ring_z(v):
    return send(v, lambda z, c, y, x: (z + 1 - 2 * c, c, y, x))


def after(value, *others):
    return lax.optimization_barrier((value, *others))


def nt(a, b, **kw):
    return lax.dot_general(
        a, b, (((1,), (1,)), ((), ())), preferred_element_type=jnp.float32, **kw
    )


def reconstruct_kernel(pieces, count, index, *refs):
    arrays = refs[:count]
    if index == 0:
        position, ra, rb, rw, own, other, tail, held, sems = refs[count:]
    else:
        position, ra, rb, rw, tail, own, other, held, sems = refs[count:]

    def copies(side):
        out = []
        for i, (a, row, rows, ry, rx, half) in enumerate(pieces):
            if half != side:
                continue
            if index == 0:
                y = lax.rem(position[1] + ry, SIDE)
                x = lax.rem(position[2] + rx, SIDE)
                to_row = pl.multiple_of((y * SIDE + x) * PART, PART)
                source = arrays[a].at[pl.ds(row, rows)]
                width = HALF
            else:
                to_row = row
                width = HALF if half == 0 else WIDE - HALF
                source = arrays[a].at[pl.ds(row, rows), pl.ds(half * HALF, width)]
            target = held.at[pl.ds(to_row, rows), pl.ds(half * HALF, width)]
            out.append(pltpu.make_async_copy(source, target, sems.at[i]))
        return out

    @pl.when(pl.program_id(0) == 0)
    def _():
        for copy in copies(0) + copies(1):
            copy.start()
        for copy in copies(0):
            copy.wait()

    val = nt(held[:, :HALF], ra[...])

    @pl.when(pl.program_id(0) == 0)
    def _():
        for copy in copies(1):
            copy.wait()

    lane = lax.broadcasted_iota(jnp.int32, (ra.shape[0], 128), 1)
    edge = rb[:, EDGE:MEANS].astype(jnp.float32)
    edge = jnp.where(lane < INSIDE, edge, 0.0).astype(jnp.bfloat16)
    val = val + nt(held[:, HALF : HALF + EDGE], rb[:, :EDGE])
    val = val + nt(held[:, HALF + EDGE : HALF + MEANS], edge)
    high, low = rw[:, :128].astype(jnp.float32), rw[:, 128:].astype(jnp.float32)

    def moved_by(means, q):
        chosen = (lane >= q * LANES) & (lane < (q + 1) * LANES)
        one = jnp.where(chosen, high, 0.0).astype(jnp.bfloat16)
        two = jnp.where(chosen, low, 0.0).astype(jnp.bfloat16)
        return nt(means, one) + nt(means, two)

    n, p = val.shape
    if index == 0:
        means = held[:, HALF + MEANS :]
        tail[...] = means
        val = val + moved_by(means, 0)
    else:
        means = tail[...]
        shift = [moved_by(means, q).reshape(16, 1, PART, p) for q in range(1, ROWS // PART)]
        val = val.reshape(16, LATE // PART, PART, p) + jnp.concatenate(shift, axis=1)
    pairs = val.reshape(SIDE, 2, n // 8, p)
    first = pairs[:, 0].reshape(n // 2, p)
    second = pairs[:, 1].reshape(n // 2, p)
    swapped = position[0] == 1
    own[...] = jnp.where(swapped, second, first)
    other[...] = jnp.where(swapped, first, second).astype(jnp.bfloat16)


def reconstruct(index, arrays, pieces, position, r, rw, tail=None):
    n = 16 * (PART if index == 0 else LATE)
    p = r.shape[0]
    half = pl.BlockSpec((n // 2, PBLOCK), lambda j: (0, j))
    whole = pl.BlockSpec((16 * PART, 128), lambda j: (0, 0))
    in_specs = [pl.BlockSpec(memory_space=pl.ANY)] * len(arrays) + [
        pl.BlockSpec(memory_space=pltpu.SMEM),
        pl.BlockSpec((PBLOCK, HALF), lambda j: (j, 0)),
        pl.BlockSpec((PBLOCK, HALF), lambda j: (j, 1)),
        pl.BlockSpec((PBLOCK, 256), lambda j: (j, 0)),
    ]
    args = [*arrays, position, r, r, rw]
    out_specs = [half, half]
    out_shape = [
        jax.ShapeDtypeStruct((n // 2, p), jnp.float32),
        jax.ShapeDtypeStruct((n // 2, p), jnp.bfloat16),
    ]
    if index == 0:
        out_specs.append(whole)
        out_shape.append(jax.ShapeDtypeStruct((16 * PART, 128), jnp.bfloat16))
    else:
        in_specs.append(whole)
        args.append(tail)
    return pl.pallas_call(
        functools.partial(reconstruct_kernel, tuple(pieces), len(arrays), index),
        grid=(pl.cdiv(p, PBLOCK),),
        in_specs=in_specs,
        out_specs=out_specs,
        out_shape=out_shape,
        scratch_shapes=[
            pltpu.VMEM((n, 2 * HALF), jnp.bfloat16),
            pltpu.SemaphoreType.DMA((len(pieces),)),
        ],
        compiler_params=pltpu.CompilerParams(vmem_limit_bytes=VMEM),
        cost_estimate=pl.CostEstimate(flops=0, bytes_accessed=0, transcendentals=0),
    )(*args)


def fit_kernel(p, *refs):
    count = len(refs) - 3
    sources, (out, held, sems) = refs[:count], refs[count:]
    copies = [
        pltpu.make_async_copy(f, held.at[i], sems.at[i]) for i, f in enumerate(sources)
    ]
    for copy in copies:
        copy.start()
    for i, copy in enumerate(copies):
        copy.wait()
        out[i] = nt(p[...], held[i]).astype(jnp.bfloat16)


def fit(points, blocks):
    n, k = points.shape
    m = blocks[0].shape[0]
    count = len(blocks)
    return pl.pallas_call(
        fit_kernel,
        in_specs=[pl.BlockSpec(memory_space=pltpu.VMEM)]
        + [pl.BlockSpec(memory_space=pl.ANY)] * count,
        out_specs=pl.BlockSpec(memory_space=pltpu.VMEM),
        out_shape=jax.ShapeDtypeStruct((count, n, m), jnp.bfloat16),
        scratch_shapes=[
            pltpu.VMEM((count, m, k), jnp.bfloat16),
            pltpu.SemaphoreType.DMA((count,)),
        ],
        compiler_params=pltpu.CompilerParams(vmem_limit_bytes=VMEM),
        cost_estimate=pl.CostEstimate(flops=0, bytes_accessed=0, transcendentals=0),
    )(points, *blocks)


def picks_by_z(own, other, z):
    got = own + swap_core(other).astype(jnp.float32)
    got = got.reshape(SIDE, 2, -1, own.shape[1])

    def pick(d):
        return lax.dynamic_index_in_dim(got, (z + d) % SIDE, 0, keepdims=False)

    return [pick(0)] + [pick(d).astype(jnp.bfloat16) for d in (1, 3, 2)]


def spread_by_z(picked):
    return picked[:1] + [send(v, hop_z(d)) for v, d in zip(picked[1:], (1, 3, 2))]


def cut(blocks, here):
    return [
        lax.dynamic_index_in_dim(blocks, (here + d) % SIDE, 1, keepdims=False)
        for d in (0, 1, 3, 2)
    ]


def owned(pieces, hop):
    return pieces[:1] + [
        send(v.astype(jnp.bfloat16), hop(d)) for v, d in zip(pieces[1:], (1, 3, 2))
    ]


def total(pieces):
    out = pieces[0].astype(jnp.float32)
    for piece in pieces[1:]:
        out = out + piece.astype(jnp.float32)
    return out


def together(*pieces):
    return jnp.concatenate(pieces, axis=0)


def per_device(slopes, valid, sensor_map, reconstructor, fitting):
    s_idx = lax.axis_index("sens")
    l_idx = lax.axis_index("layer")
    z, c = s_idx // 2, s_idx % 2
    y, x = l_idx // SIDE, l_idx % SIDE
    width = slopes.shape[1]
    width_p = reconstructor.shape[0]
    act = fitting.shape[0]
    position = jnp.stack([c, y, x]).astype(jnp.int32)

    live = valid.astype(jnp.bfloat16)[None, :]
    masked = slopes * live
    late = lax.all_gather(
        jnp.pad(masked[PART:], ((0, 0), (0, WIDE - width))), "layer", axis=0, tiled=True
    )

    own_a = masked[:PART, :HALF]
    a_l, a_r = right(own_a), left(own_a)
    a_d, a_u = up(own_a), down(own_a)
    fits = [fitting, ring_z(fitting)]

    group = sensor_map * 2 + (lax.iota(jnp.int32, width) + s_idx * width) % 2
    lane = lax.iota(jnp.int32, 128)
    label = jnp.where(lane < LANES * (ROWS // PART), lane % 12, -1)
    member = ((group[None, :] == label[:, None]) & (valid[None, :] == 1)).astype(jnp.bfloat16)
    counted = jnp.concatenate([masked, jnp.ones((8, width), jnp.bfloat16)], axis=0)
    stats = nt(counted, member)
    stats = jnp.broadcast_to(stats[None], (8, *stats.shape))
    stats = jnp.sum(lax.all_to_all(stats, "sens", 0, 0, tiled=True), axis=0)
    means = stats[:ROWS] / jnp.maximum(stats[ROWS : ROWS + 1], 1.0)
    high = lax.reduce_precision(means, 8, 7)
    means = jnp.where((lane % LANES < 12)[None, :], high, means - high)
    means = sum(
        jnp.where((lane // LANES == q)[None, :], means[q * PART : (q + 1) * PART], 0.0)
        for q in range(ROWS // PART)
    ).astype(jnp.bfloat16)
    own_b = jnp.pad(masked[:PART, HALF:], ((0, 0), (0, 2 * HALF - width)))
    own_b = own_b + jnp.pad(means, ((0, 0), (MEANS, 0)))
    b_l, b_r = right(own_b), left(own_b)
    b_d, b_u = up(own_b), down(own_b)

    send_u = together(a_l, a_r, a_d)
    send_d = together(a_l, a_r, b_u)
    send_r = together(b_d, b_u, a_l)
    send_l = together(b_d, b_u, b_r)
    fits[1], member, send_u, send_d, send_r, send_l, a_u, b_l = after(
        fits[1], member, send_u, send_d, send_r, send_l, a_u, b_l
    )
    fits.append(ring_z(fits[-1]))
    one_d, one_u = up(send_u), down(send_d)
    one_l, one_r = right(send_r), left(send_l)

    rw = -nt(reconstructor, member)
    rw_high = lax.reduce_precision(rw, 8, 7)
    rw_low = jnp.where((lane % LANES < 12)[None, :], rw - rw_high, 0.0)
    rw = jnp.concatenate([rw_high, rw_low], axis=1).astype(jnp.bfloat16)

    rw, fits[2], one_d, one_u, one_l, one_r = after(
        rw, fits[2], one_d, one_u, one_l, one_r
    )
    fits.append(ring_z(fits[-1]))
    far_x_a, far_y_b = one_l[2 * PART :], one_u[2 * PART :]
    two_d = together(far_x_a, one_d[:PART])
    two_u = together(far_x_a, one_u[PART : 2 * PART])
    two_l = together(far_y_b, one_l[:PART])
    two_r = together(far_y_b, one_r[PART : 2 * PART])
    two_d, two_u, two_l, two_r = after(two_d, two_u, two_l, two_r)
    get_d, get_u = up(two_d), down(two_u)
    get_l, get_r = right(two_l), left(two_r)

    get_u, get_r, *ends = after(get_u, get_r, get_d[:PART], get_l[:PART])
    end_d, end_l = up(ends[0]), right(ends[1])
    end_d, end_l, *fits = after(end_d, end_l, *fits)

    arrays = [own_a, own_b, a_l, b_l, a_r, b_r, a_d, b_d, a_u, b_u, one_d, one_u, one_l, one_r]
    arrays += [get_d, get_u, get_l, get_r, end_d, end_l]

    def piece(array, block, ry, rx, side):
        index = [i for i, a in enumerate(arrays) if a is array][0]
        return (index, block * PART, PART, ry, rx, side)

    pieces = []
    for ry, rx, (array_a, block_a), (array_b, block_b) in (
        (0, 0, (own_a, 0), (own_b, 0)),
        (0, 3, (a_l, 0), (b_l, 0)),
        (0, 1, (a_r, 0), (b_r, 0)),
        (3, 0, (a_d, 0), (b_d, 0)),
        (1, 0, (a_u, 0), (b_u, 0)),
        (3, 3, (one_d, 0), (one_l, 0)),
        (3, 1, (one_d, 1), (one_r, 0)),
        (1, 3, (one_u, 0), (one_l, 1)),
        (1, 1, (one_u, 1), (one_r, 1)),
        (0, 2, (one_l, 2), (one_r, 2)),
        (2, 0, (one_d, 2), (one_u, 2)),
        (3, 2, (get_d, 0), (get_l, 1)),
        (1, 2, (get_u, 0), (get_r, 1)),
        (2, 3, (get_d, 1), (get_l, 0)),
        (2, 1, (get_u, 1), (get_r, 0)),
        (2, 2, (end_d, 0), (end_l, 0)),
    ):
        pieces.append(piece(array_a, block_a, ry, rx, 0))
        pieces.append(piece(array_b, block_b, ry, rx, 1))
    own, other, tail = reconstruct(0, arrays, pieces, position, reconstructor, rw)
    swapped = [swap_core(f) for f in fits]
    own, other, *swapped = after(own, other, *swapped)
    picked = picks_by_z(own, other, z)
    terms = spread_by_z(picked)
    terms[0], late = after(terms[0], late)
    near = total(terms).astype(jnp.bfloat16)

    own, other = reconstruct(
        1, [late], [(0, 0, 16 * LATE, 0, 0, side) for side in (0, 1)],
        position, reconstructor, rw, tail,
    )
    own, other, near = after(own, other, near)
    far = total(spread_by_z(picks_by_z(own, other, z))).astype(jnp.bfloat16)
    points = jnp.concatenate([near, far], axis=1)

    rows = points.reshape(SIDE, SIDE, 8, width_p)
    rows = jnp.where(c == 0, rows, jnp.swapaxes(rows, 0, 1)).reshape(2 * ROWS, width_p)
    one = jnp.where(c == 0, y, x)
    two = jnp.where(c == 0, x, y)
    half_a = cut(fit(rows, fits).reshape(4, SIDE, SIDE * 8, act), one)
    half_a = owned(half_a, hop_one)
    half_b = cut(fit(rows, swapped).reshape(4, SIDE, SIDE * 8, act), one)
    half_b = owned(half_b, hop_one)
    both = jnp.concatenate([total(half_a), total(half_b)], axis=0)
    done = total(owned(cut(both.reshape(8, SIDE, 8, act), two), hop_two))

    sens = lax.iota(jnp.int32, 8)
    step = jnp.where(sens % 2 == 0, z - sens // 2, sens // 2 - z) % SIDE
    found = jnp.where(sens % 2 == c, 0, 4) + step
    done = jnp.take(done, found, axis=0, mode="clip")
    return jnp.moveaxis(done, 0, 1).reshape(8, 8 * act)


def solution(mesh):
    placed = (P("layer", "sens"), P("sens"), P("sens"), P("layer", "sens"), P("sens", "layer"))
    return jax.shard_map(
        per_device,
        mesh=mesh,
        in_specs=placed,
        out_specs=P(("sens", "layer"), None),
        check_vma=False,
    )
```

```python
import functools

import jax
import jax.numpy as jnp
from jax import lax
from jax.experimental import pallas as pl
from jax.experimental.pallas import tpu as pltpu
from jax.sharding import PartitionSpec as P

SENSORS = 6
AXES = ("sens", "layer")
SIDE = 4
ROWS = 64
PART = 16
LATE = ROWS - PART
LANES = 24
HALF = 4096
EDGE = 3840
MEANS = 3968
WIDE = 8064
INSIDE = 14
PBLOCK = 256
VMEM = 52 * 2**20


def moved(fn):
    pairs = []
    for z in range(4):
        for c in range(2):
            for y in range(4):
                for x in range(4):
                    z2, c2, y2, x2 = fn(z, c, y, x)
                    pairs.append(
                        ((z * 2 + c) * 16 + y * 4 + x,
                         ((z2 % 4) * 2 + c2 % 2) * 16 + (y2 % 4) * 4 + x2 % 4)
                    )
    return pairs


def send(x, fn):
    return lax.ppermute(x, AXES, moved(fn))


def swap_core(v):
    return send(v, lambda z, c, y, x: (z, c + 1, y, x))


def right(v):
    return send(v, lambda z, c, y, x: (z, c, y, x + 1))


def left(v):
    return send(v, lambda z, c, y, x: (z, c, y, x - 1))


def up(v):
    return send(v, lambda z, c, y, x: (z, c, y + 1, x))


def down(v):
    return send(v, lambda z, c, y, x: (z, c, y - 1, x))


def hop_z(d):
    return lambda z, c, y, x: (z + d, c, y, x)


def hop_one(d):
    return lambda z, c, y, x: (z, c, y + d * (1 - c), x + d * c)


def hop_two(d):
    return lambda z, c, y, x: (z, c, y + d * c, x + d * (1 - c))


def ring_z(v):
    return send(v, lambda z, c, y, x: (z + 1 - 2 * c, c, y, x))


def after(value, *others):
    return lax.optimization_barrier((value, *others))


def nt(a, b, **kw):
    return lax.dot_general(
        a, b, (((1,), (1,)), ((), ())), preferred_element_type=jnp.float32, **kw
    )


def reconstruct_kernel(pieces, count, index, *refs):
    arrays = refs[:count]
    if index == 0:
        position, ra, rb, rw, own, other, tail, held, sems = refs[count:]
    else:
        position, ra, rb, rw, tail, own, other, held, sems = refs[count:]

    def copies(side):
        out = []
        for i, (a, row, rows, ry, rx, half) in enumerate(pieces):
            if half != side:
                continue
            if index == 0:
                y = lax.rem(position[1] + ry, SIDE)
                x = lax.rem(position[2] + rx, SIDE)
                to_row = pl.multiple_of((y * SIDE + x) * PART, PART)
                source = arrays[a].at[pl.ds(row, rows)]
                width = HALF
            else:
                to_row = row
                width = HALF if half == 0 else WIDE - HALF
                source = arrays[a].at[pl.ds(row, rows), pl.ds(half * HALF, width)]
            target = held.at[pl.ds(to_row, rows), pl.ds(half * HALF, width)]
            out.append(pltpu.make_async_copy(source, target, sems.at[i]))
        return out

    @pl.when(pl.program_id(0) == 0)
    def _():
        for copy in copies(0) + copies(1):
            copy.start()
        for copy in copies(0):
            copy.wait()

    val = nt(held[:, :HALF], ra[...])

    @pl.when(pl.program_id(0) == 0)
    def _():
        for copy in copies(1):
            copy.wait()

    lane = lax.broadcasted_iota(jnp.int32, (ra.shape[0], 128), 1)
    edge = rb[:, EDGE:MEANS].astype(jnp.float32)
    edge = jnp.where(lane < INSIDE, edge, 0.0).astype(jnp.bfloat16)
    val = val + nt(held[:, HALF : HALF + EDGE], rb[:, :EDGE])
    val = val + nt(held[:, HALF + EDGE : HALF + MEANS], edge)
    high, low = rw[:, :128].astype(jnp.float32), rw[:, 128:].astype(jnp.float32)

    def moved_by(means, q):
        chosen = (lane >= q * LANES) & (lane < (q + 1) * LANES)
        one = jnp.where(chosen, high, 0.0).astype(jnp.bfloat16)
        two = jnp.where(chosen, low, 0.0).astype(jnp.bfloat16)
        return nt(means, one) + nt(means, two)

    n, p = val.shape
    if index == 0:
        means = held[:, HALF + MEANS :]
        tail[...] = means
        val = val + moved_by(means, 0)
    else:
        means = tail[...]
        shift = [moved_by(means, q).reshape(16, 1, PART, p) for q in range(1, ROWS // PART)]
        val = val.reshape(16, LATE // PART, PART, p) + jnp.concatenate(shift, axis=1)
    pairs = val.reshape(SIDE, 2, n // 8, p)
    first = pairs[:, 0].reshape(n // 2, p)
    second = pairs[:, 1].reshape(n // 2, p)
    swapped = position[0] == 1
    own[...] = jnp.where(swapped, second, first)
    other[...] = jnp.where(swapped, first, second).astype(jnp.bfloat16)


def reconstruct(index, arrays, pieces, position, r, rw, tail=None):
    n = 16 * (PART if index == 0 else LATE)
    p = r.shape[0]
    half = pl.BlockSpec((n // 2, PBLOCK), lambda j: (0, j))
    whole = pl.BlockSpec((16 * PART, 128), lambda j: (0, 0))
    in_specs = [pl.BlockSpec(memory_space=pl.ANY)] * len(arrays) + [
        pl.BlockSpec(memory_space=pltpu.SMEM),
        pl.BlockSpec((PBLOCK, HALF), lambda j: (j, 0)),
        pl.BlockSpec((PBLOCK, HALF), lambda j: (j, 1)),
        pl.BlockSpec((PBLOCK, 256), lambda j: (j, 0)),
    ]
    args = [*arrays, position, r, r, rw]
    out_specs = [half, half]
    out_shape = [
        jax.ShapeDtypeStruct((n // 2, p), jnp.float32),
        jax.ShapeDtypeStruct((n // 2, p), jnp.bfloat16),
    ]
    if index == 0:
        out_specs.append(whole)
        out_shape.append(jax.ShapeDtypeStruct((16 * PART, 128), jnp.bfloat16))
    else:
        in_specs.append(whole)
        args.append(tail)
    return pl.pallas_call(
        functools.partial(reconstruct_kernel, tuple(pieces), len(arrays), index),
        grid=(pl.cdiv(p, PBLOCK),),
        in_specs=in_specs,
        out_specs=out_specs,
        out_shape=out_shape,
        scratch_shapes=[
            pltpu.VMEM((n, 2 * HALF), jnp.bfloat16),
            pltpu.SemaphoreType.DMA((len(pieces),)),
        ],
        compiler_params=pltpu.CompilerParams(vmem_limit_bytes=VMEM),
        cost_estimate=pl.CostEstimate(flops=0, bytes_accessed=0, transcendentals=0),
    )(*args)


def fit_kernel(p, *refs):
    count = len(refs) - 3
    sources, (out, held, sems) = refs[:count], refs[count:]
    copies = [
        pltpu.make_async_copy(f, held.at[i], sems.at[i]) for i, f in enumerate(sources)
    ]
    for copy in copies:
        copy.start()
    for i, copy in enumerate(copies):
        copy.wait()
        out[i] = nt(p[...], held[i]).astype(jnp.bfloat16)


def fit(points, blocks):
    n, k = points.shape
    m = blocks[0].shape[0]
    count = len(blocks)
    return pl.pallas_call(
        fit_kernel,
        in_specs=[pl.BlockSpec(memory_space=pltpu.VMEM)]
        + [pl.BlockSpec(memory_space=pl.ANY)] * count,
        out_specs=pl.BlockSpec(memory_space=pltpu.VMEM),
        out_shape=jax.ShapeDtypeStruct((count, n, m), jnp.bfloat16),
        scratch_shapes=[
            pltpu.VMEM((count, m, k), jnp.bfloat16),
            pltpu.SemaphoreType.DMA((count,)),
        ],
        compiler_params=pltpu.CompilerParams(vmem_limit_bytes=VMEM),
        cost_estimate=pl.CostEstimate(flops=0, bytes_accessed=0, transcendentals=0),
    )(points, *blocks)


def picks_by_z(own, other, z):
    got = own + swap_core(other).astype(jnp.float32)
    got = got.reshape(SIDE, 2, -1, own.shape[1])

    def pick(d):
        return lax.dynamic_index_in_dim(got, (z + d) % SIDE, 0, keepdims=False)

    return [pick(0)] + [pick(d).astype(jnp.bfloat16) for d in (1, 3, 2)]


def spread_by_z(picked):
    return picked[:1] + [send(v, hop_z(d)) for v, d in zip(picked[1:], (1, 3, 2))]


def cut(blocks, here):
    return [
        lax.dynamic_index_in_dim(blocks, (here + d) % SIDE, 1, keepdims=False)
        for d in (0, 1, 3, 2)
    ]


def owned(pieces, hop):
    return pieces[:1] + [
        send(v.astype(jnp.bfloat16), hop(d)) for v, d in zip(pieces[1:], (1, 3, 2))
    ]


def total(pieces):
    out = pieces[0].astype(jnp.float32)
    for piece in pieces[1:]:
        out = out + piece.astype(jnp.float32)
    return out


def together(*pieces):
    return jnp.concatenate(pieces, axis=0)


def per_device(slopes, valid, sensor_map, reconstructor, fitting):
    s_idx = lax.axis_index("sens")
    l_idx = lax.axis_index("layer")
    z, c = s_idx // 2, s_idx % 2
    y, x = l_idx // SIDE, l_idx % SIDE
    width = slopes.shape[1]
    width_p = reconstructor.shape[0]
    act = fitting.shape[0]
    position = jnp.stack([c, y, x]).astype(jnp.int32)

    live = valid.astype(jnp.bfloat16)[None, :]
    masked = slopes * live
    late = lax.all_gather(
        jnp.pad(masked[PART:], ((0, 0), (0, WIDE - width))), "layer", axis=0, tiled=True
    )

    own_a = masked[:PART, :HALF]
    a_l, a_r = right(own_a), left(own_a)
    a_d, a_u = up(own_a), down(own_a)
    fits = [fitting, ring_z(fitting)]

    group = sensor_map * 2 + (lax.iota(jnp.int32, width) + s_idx * width) % 2
    lane = lax.iota(jnp.int32, 128)
    label = jnp.where(lane < LANES * (ROWS // PART), lane % 12, -1)
    member = ((group[None, :] == label[:, None]) & (valid[None, :] == 1)).astype(jnp.bfloat16)
    counted = jnp.concatenate([masked, jnp.ones((8, width), jnp.bfloat16)], axis=0)
    stats = nt(counted, member)
    stats = jnp.broadcast_to(stats[None], (8, *stats.shape))
    stats = jnp.sum(lax.all_to_all(stats, "sens", 0, 0, tiled=True), axis=0)
    means = stats[:ROWS] / jnp.maximum(stats[ROWS : ROWS + 1], 1.0)
    high = lax.reduce_precision(means, 8, 7)
    means = jnp.where((lane % LANES < 12)[None, :], high, means - high)
    means = sum(
        jnp.where((lane // LANES == q)[None, :], means[q * PART : (q + 1) * PART], 0.0)
        for q in range(ROWS // PART)
    ).astype(jnp.bfloat16)
    own_b = jnp.pad(masked[:PART, HALF:], ((0, 0), (0, 2 * HALF - width)))
    own_b = own_b + jnp.pad(means, ((0, 0), (MEANS, 0)))
    b_l, b_r = right(own_b), left(own_b)
    b_d, b_u = up(own_b), down(own_b)

    send_u = together(a_l, a_r, a_d)
    send_d = together(a_l, a_r, b_u)
    send_r = together(b_d, b_u, a_l)
    send_l = together(b_d, b_u, b_r)
    member, send_u, send_d, send_r, send_l, a_u, b_l = after(
        member, send_u, send_d, send_r, send_l, a_u, b_l
    )
    one_d, one_u = up(send_u), down(send_d)
    one_l, one_r = right(send_r), left(send_l)

    fits[1], member = after(fits[1], member)
    fits.append(ring_z(fits[-1]))
    rw = -nt(reconstructor, member)
    rw_high = lax.reduce_precision(rw, 8, 7)
    rw_low = jnp.where((lane % LANES < 12)[None, :], rw - rw_high, 0.0)
    rw = jnp.concatenate([rw_high, rw_low], axis=1).astype(jnp.bfloat16)

    rw, one_d, one_u, one_l, one_r = after(rw, one_d, one_u, one_l, one_r)
    far_x_a, far_y_b = one_l[2 * PART :], one_u[2 * PART :]
    two_d = together(far_x_a, one_d[:PART])
    two_u = together(far_x_a, one_u[PART : 2 * PART])
    two_l = together(far_y_b, one_l[:PART])
    two_r = together(far_y_b, one_r[PART : 2 * PART])
    two_d, two_u, two_l, two_r = after(two_d, two_u, two_l, two_r)
    get_d, get_u = up(two_d), down(two_u)
    get_l, get_r = right(two_l), left(two_r)

    get_u, get_r, *ends = after(get_u, get_r, get_d[:PART], get_l[:PART])
    end_d, end_l = up(ends[0]), right(ends[1])
    end_d, end_l, *fits[:2] = after(end_d, end_l, *fits[:2])

    arrays = [own_a, own_b, a_l, b_l, a_r, b_r, a_d, b_d, a_u, b_u, one_d, one_u, one_l, one_r]
    arrays += [get_d, get_u, get_l, get_r, end_d, end_l]

    def piece(array, block, ry, rx, side):
        index = [i for i, a in enumerate(arrays) if a is array][0]
        return (index, block * PART, PART, ry, rx, side)

    pieces = []
    for ry, rx, (array_a, block_a), (array_b, block_b) in (
        (0, 0, (own_a, 0), (own_b, 0)),
        (0, 3, (a_l, 0), (b_l, 0)),
        (0, 1, (a_r, 0), (b_r, 0)),
        (3, 0, (a_d, 0), (b_d, 0)),
        (1, 0, (a_u, 0), (b_u, 0)),
        (3, 3, (one_d, 0), (one_l, 0)),
        (3, 1, (one_d, 1), (one_r, 0)),
        (1, 3, (one_u, 0), (one_l, 1)),
        (1, 1, (one_u, 1), (one_r, 1)),
        (0, 2, (one_l, 2), (one_r, 2)),
        (2, 0, (one_d, 2), (one_u, 2)),
        (3, 2, (get_d, 0), (get_l, 1)),
        (1, 2, (get_u, 0), (get_r, 1)),
        (2, 3, (get_d, 1), (get_l, 0)),
        (2, 1, (get_u, 1), (get_r, 0)),
        (2, 2, (end_d, 0), (end_l, 0)),
    ):
        pieces.append(piece(array_a, block_a, ry, rx, 0))
        pieces.append(piece(array_b, block_b, ry, rx, 1))
    own, other, tail = reconstruct(0, arrays, pieces, position, reconstructor, rw)
    swapped = [swap_core(f) for f in fits[:2]]
    own, other, fits[2], *swapped = after(own, other, fits[2], *swapped)
    fits.append(ring_z(fits[-1]))
    picked = picks_by_z(own, other, z)
    terms = spread_by_z(picked)
    terms[0], late = after(terms[0], late)
    near = total(terms).astype(jnp.bfloat16)

    own, other = reconstruct(
        1, [late], [(0, 0, 16 * LATE, 0, 0, side) for side in (0, 1)],
        position, reconstructor, rw, tail,
    )
    own, other, near, *fits[2:] = after(own, other, near, *fits[2:])
    swapped += [swap_core(f) for f in fits[2:]]
    far = total(spread_by_z(picks_by_z(own, other, z))).astype(jnp.bfloat16)
    points = jnp.concatenate([near, far], axis=1)

    rows = points.reshape(SIDE, SIDE, 8, width_p)
    rows = jnp.where(c == 0, rows, jnp.swapaxes(rows, 0, 1)).reshape(2 * ROWS, width_p)
    one = jnp.where(c == 0, y, x)
    two = jnp.where(c == 0, x, y)
    half_a = cut(fit(rows, fits).reshape(4, SIDE, SIDE * 8, act), one)
    half_a = owned(half_a, hop_one)
    half_b = cut(fit(rows, swapped).reshape(4, SIDE, SIDE * 8, act), one)
    half_b = owned(half_b, hop_one)
    both = jnp.concatenate([total(half_a), total(half_b)], axis=0)
    done = total(owned(cut(both.reshape(8, SIDE, 8, act), two), hop_two))

    sens = lax.iota(jnp.int32, 8)
    step = jnp.where(sens % 2 == 0, z - sens // 2, sens // 2 - z) % SIDE
    found = jnp.where(sens % 2 == c, 0, 4) + step
    done = jnp.take(done, found, axis=0, mode="clip")
    return jnp.moveaxis(done, 0, 1).reshape(8, 8 * act)


def solution(mesh):
    placed = (P("layer", "sens"), P("sens"), P("sens"), P("layer", "sens"), P("sens", "layer"))
    return jax.shard_map(
        per_device,
        mesh=mesh,
        in_specs=placed,
        out_specs=P(("sens", "layer"), None),
        check_vma=False,
    )
```
